512 devices in a mesh: ctx: 64 (over x, y, core), head: 8 (over z).
Axes of the slice: x: 4, y: 8, z: 8, core: 2. Of those that a mesh axis runs over, the one named last changes fastest.
Arguments:
- hidden_in: bfloat16 [16384, 4096], P('ctx', 'head'), may hold values from -6 to 6
- proj_weights: bfloat16 [3, 4096, 16, 128], P(None, None, 'head', 'ctx'), may hold values from -0.09375 to 0.09375
- directions: bfloat16 [3, 4096, 16, 128], P(None, None, 'head', 'ctx'), may hold values from -6 to 6
Outputs:
- attn_out: bfloat16 [2, 16384, 16, 128], P(None, 'ctx', 'head')
The draws below stay inside these ranges and needn't reach their ends.
All inputs are finite; a program needn't handle non-finite values.
Results may differ from the reference program's by a relative error of at most 0.011.
Values may be sent and summed in bfloat16 or wider, within the bound.
No kernel may reach another device: no remote copies, remote signals or barrier semaphores. Data moves between devices by JAX's collectives and lax.ppermute only.
A program may use at most 64 MiB of HBM per device.

```python
import jax
import jax.numpy as jnp
from jax import lax

D = 4096
HEADS = 16
HD = 128
TOK_DEV = 256
TOKENS = 16384


def shard_levels(rng, dims, pieces, smallest, top_value):
    def one(position, shards_of):
        heights = jax.random.uniform(jax.random.fold_in(jax.random.fold_in(rng, 6), position), (shards_of,), jnp.float32, smallest / len(pieces), top_value / len(pieces))
        return jnp.repeat(jnp.exp(heights), dims[position] // shards_of).reshape((-1,) + (1,) * (len(dims) - position - 1))

    gain = one(*pieces[0])
    for cut in pieces[1:]:
        gain = gain * one(*cut)
    return gain


def centred(stream_key, shape, spread, reach, pieces=(), kind=jnp.bfloat16):
    drawn = spread * jax.random.normal(stream_key, shape, jnp.float32)
    if pieces:
        drawn = drawn * shard_levels(stream_key, shape, pieces, -0.22, 0.18)
    return jnp.clip(drawn, -reach, reach).astype(kind)


def setup_inputs(seed: int = 0) -> dict:
    splits = jax.random.split(jax.random.key(seed), 4)
    hidden_in = centred(splits[0], (TOKENS, D), 1.0, 6.0, ((0, 64), (1, 8)))
    proj_weights = centred(splits[1], (3, D, HEADS, HD), D ** -0.5, 0.09375, ((2, 8), (3, 64)))
    directions = centred(splits[2], (3, D, HEADS, HD), 1.0, 6.0, ((2, 8), (3, 64)))
    return dict(hidden_in=hidden_in, proj_weights=proj_weights, directions=directions)


def one_block(packed):
    query_rows, key_rows, value_rows, prior_state = packed
    scores = jnp.einsum('sthe,suhe->shtu', query_rows, key_rows)
    row_index = lax.broadcasted_iota(jnp.int32, (query_rows.shape[1], query_rows.shape[1]), 0)
    col_index = lax.broadcasted_iota(jnp.int32, (query_rows.shape[1], query_rows.shape[1]), 1)
    masked = jnp.where(col_index <= row_index, scores, jnp.float32(0.0))
    attn_weights = lax.optimization_barrier(masked.astype(jnp.bfloat16)).astype(jnp.float32)
    inner_part = jnp.einsum('shtu,suhe->sthe', attn_weights, value_rows)
    carried = lax.optimization_barrier(prior_state.astype(jnp.bfloat16)).astype(jnp.float32)
    cross_part = jnp.einsum('sthe,shef->sthf', query_rows, carried)
    combined = inner_part + cross_part
    normed = combined * lax.rsqrt(lax.optimization_barrier(jnp.mean(combined * combined, axis=-1, keepdims=True)) + 1e-05)
    return normed.astype(jnp.bfloat16)

def reference(hidden_in, proj_weights, directions):
    step_size = 0.1 * D ** (-0.5)
    tokens = hidden_in.astype(jnp.float32)
    base_out = jnp.einsum('td,mdhe->mthe', tokens, proj_weights.astype(jnp.float32))
    direct_out = jnp.einsum('td,mdhe->mthe', tokens, directions.astype(jnp.float32))
    sign_pair = jnp.array([1.0, -1.0], jnp.float32) * jnp.float32(step_size)
    signed = (base_out[None] + sign_pair[:, None, None, None, None] * direct_out[None]).astype(jnp.bfloat16)
    blocks = TOKENS // TOK_DEV
    shaped = signed.astype(jnp.float32).reshape(2, 3, blocks, TOK_DEV, HEADS, HD)
    query_rows = shaped[:, 0]
    key_rows = shaped[:, 1]
    value_rows = shaped[:, 2]
    block_state = jnp.einsum('sbthe,sbthf->sbhef', key_rows, value_rows)
    running = jnp.cumsum(block_state, axis=1)
    prior_state = jnp.concatenate([jnp.zeros_like(running[:, :1]), running[:, :-1]], axis=1)
    results = lax.map(one_block, (jnp.moveaxis(query_rows, 1, 0), jnp.moveaxis(key_rows, 1, 0), jnp.moveaxis(value_rows, 1, 0), jnp.moveaxis(prior_state, 1, 0)))
    return jnp.moveaxis(results, 0, 1).reshape(2, TOKENS, HEADS, HD)
```

```python
import functools

import jax
import jax.numpy as jnp
from jax import lax
from jax.experimental import pallas as pl
from jax.experimental.pallas import tpu as pltpu
from jax.sharding import Mesh
from jax.sharding import PartitionSpec as P

NX, NY, NC, NZ = 4, 8, 2, 8
TOK, HD, PIECE = 256, 128, 512
D = NZ * PIECE
STEP = 0.1 * D ** (-0.5)
F32, BF16 = jnp.float32, jnp.bfloat16


def replicate(x, n):
    return jnp.broadcast_to(x[None], (n,) + x.shape)


def exchange(x, axes):
    return lax.all_to_all(x, axes, 0, 0, tiled=True)


def signs_and_order(acc, kinds, x_major):
    cols = acc.shape[1]
    lane = lax.broadcasted_iota(jnp.int32, acc.shape, 1)
    left = pltpu.roll(acc, cols - 2, 1)
    right = pltpu.roll(acc, 2, 1)
    step = jnp.float32(STEP)
    signed = jnp.where((lane & 3) < 2, acc + step * left, right + (-step) * acc).astype(BF16)
    row = lax.broadcasted_iota(jnp.int32, (cols, cols), 0)
    col = lax.broadcasted_iota(jnp.int32, (cols, cols), 1)
    j = row & 1
    sign = (row >> 1) & 1
    kind = (row >> 2) & (kinds - 1)
    rest = row >> (2 + (kinds - 1))
    core = rest & 1
    chip = rest >> 1
    if not x_major:
        chip = (chip & (NX - 1)) * NY + (chip >> 2)
    target = (kind * 2 + sign) * HD + (chip * 2 + core) * 2 + j
    pick = jnp.where(col == target, jnp.float32(1.0), jnp.float32(0.0)).astype(BF16)
    return jnp.dot(signed, pick, preferred_element_type=F32).astype(BF16)


NT = (((1,), (1,)), ((), ()))
TN = (((0,), (0,)), ((), ()))


def accumulate(own_ref, other_ref, weight_ref, acc):
    @pl.when(pl.program_id(0) == 0)
    def _():
        acc[...] = jnp.zeros_like(acc)

    weight = weight_ref[...]
    for block, ref in enumerate((own_ref, other_ref)):
        acc[block] += lax.dot_general(ref[0], weight, NT, preferred_element_type=F32)


def query_kernel(own_ref, other_ref, weight_ref, out_ref, acc):
    accumulate(own_ref, other_ref, weight_ref, acc)

    @pl.when(pl.program_id(0) == NZ - 1)
    def _():
        for block in range(2):
            rows = signs_and_order(acc[block], 1, True)
            for s in range(2):
                out_ref[block, s] = rows[:, s * HD : (s + 1) * HD]


def key_value_kernel(own_ref, other_ref, weight_ref, out_ref, state_ref, total_ref, acc):
    accumulate(own_ref, other_ref, weight_ref, acc)

    @pl.when(pl.program_id(0) == NZ - 1)
    def _():
        for block in range(2):
            rows = signs_and_order(acc[block], 2, False)
            for s in range(2):
                key = rows[:, s * HD : (s + 1) * HD]
                value = rows[:, (2 + s) * HD : (3 + s) * HD]
                out_ref[0, block, s] = key
                out_ref[1, block, s] = value
                state_ref[block, s] = lax.dot_general(key, value, TN, preferred_element_type=F32)
        total_ref[...] = (state_ref[0] + state_ref[1]).astype(BF16)


def project(kernel, own, other, weight, out_shape):
    rows = weight.shape[0]
    piece = pl.BlockSpec((1, TOK, PIECE), lambda k: (k, 0, 0))
    whole = jax.tree.map(lambda s: pl.BlockSpec(s.shape, lambda k, n=len(s.shape): (0,) * n), out_shape)
    return pl.pallas_call(
        kernel,
        grid=(NZ,),
        in_specs=[piece, piece, pl.BlockSpec((rows, PIECE), lambda k: (0, k))],
        out_specs=whole,
        out_shape=out_shape,
        scratch_shapes=[pltpu.VMEM((2, TOK, rows), F32)],
        compiler_params=pltpu.CompilerParams(
            dimension_semantics=("arbitrary",), vmem_limit_bytes=32 << 20
        ),
    )(own, other, weight)


def inner_kernel(query_ref, kv_ref, out_ref):
    row = lax.broadcasted_iota(jnp.int32, (TOK, TOK), 0)
    col = lax.broadcasted_iota(jnp.int32, (TOK, TOK), 1)
    for block in range(2):
        for s in range(2):
            scores = lax.dot_general(
                query_ref[block, s], kv_ref[0, block, s], NT, preferred_element_type=F32
            )
            weights = jnp.where(col <= row, scores, 0.0).astype(BF16)
            out_ref[block, s] = jnp.dot(weights, kv_ref[1, block, s], preferred_element_type=F32)


def cross_kernel(query_ref, inner_ref, state_ref, partial_ref, out_ref):
    core = lax.axis_index("c")
    prior = jnp.sum(partial_ref[...].astype(F32), axis=0)
    for block in range(2):
        later = jnp.where(core == (1 - block), jnp.float32(1.0), jnp.float32(0.0))
        for s in range(2):
            carried = (prior[s] + later * state_ref[1 - block, s]).astype(BF16)
            combined = inner_ref[block, s] + jnp.dot(
                query_ref[block, s], carried, preferred_element_type=F32
            )
            scale = lax.rsqrt(jnp.mean(combined * combined, axis=-1, keepdims=True) + 1e-05)
            out_ref[block, s] = (combined * scale).astype(BF16)


def call(kernel, out_shape, *args):
    return pl.pallas_call(
        kernel,
        out_shape=out_shape,
        in_specs=[pl.BlockSpec(memory_space=pltpu.VMEM)] * len(args),
        out_specs=pl.BlockSpec(memory_space=pltpu.VMEM),
        compiler_params=pltpu.CompilerParams(vmem_limit_bytes=32 << 20),
    )(*args)


def shape(*dims, dtype=BF16):
    return jax.ShapeDtypeStruct(dims, dtype)


def on_device(hidden_in, proj_weights, directions):
    x, y, c = (lax.axis_index(name) for name in "xyc")
    swap = [(0, 1), (1, 0)]

    both = jnp.stack(
        [jnp.transpose(proj_weights, (0, 2, 3, 1)), jnp.transpose(directions, (0, 2, 3, 1))], axis=2
    )
    kv_rows = jnp.transpose(both[1:], (1, 0, 2, 3, 4)).reshape(NC, 8, D)
    q_rows = both[0].reshape(NC, 4, D)

    own = exchange(replicate(hidden_in, NZ), "z")
    kv_part = exchange(replicate(kv_rows, NX).reshape(NX * NC, 8, D), ("x", "c"))
    q_part = exchange(replicate(q_rows, NY).reshape(NY * NC, 4, D), ("y", "c"))
    kv_weight = lax.all_gather(kv_part.reshape(64, D), "y", axis=0, tiled=True)
    q_weight = exchange(replicate(q_part.reshape(64, D), NX), "x").reshape(256, D)
    other = lax.ppermute(own, "c", swap)

    query = project(query_kernel, own, other, q_weight, shape(2, 2, TOK, HD))
    kv, state, total = project(
        key_value_kernel,
        own,
        other,
        kv_weight,
        (shape(2, 2, 2, TOK, HD), shape(2, 2, HD, HD, dtype=F32), shape(2, HD, HD)),
    )

    over_x = exchange(replicate(total, NX), "x")
    before = (jnp.arange(NX) < x).astype(F32)
    earlier = jnp.sum(over_x.astype(F32) * before[:, None, None, None], axis=0)
    later = (jnp.arange(NY) > y).astype(F32)
    sent = earlier[None] + later[:, None, None, None] * (state[0] + state[1])[None]
    partial = exchange(sent.astype(BF16), "y")

    inner = call(inner_kernel, shape(2, 2, TOK, HD, dtype=F32), query, kv)
    out = call(cross_kernel, shape(2, 2, TOK, HD), query, inner, state, partial)
    mine, theirs = out[0], lax.ppermute(out[1], "c", swap)
    first = jnp.where(c == 0, mine, theirs)
    second = jnp.where(c == 0, theirs, mine)
    return jnp.stack([first, second], axis=2)


def solution(mesh):
    mesh4 = Mesh(mesh.devices.reshape(NX, NY, NC, NZ), ("x", "y", "c", "z"))
    ctx = ("x", "y", "c")
    return jax.shard_map(
        on_device,
        mesh=mesh4,
        in_specs=(P(ctx, "z"), P(None, None, "z", ctx), P(None, None, "z", ctx)),
        out_specs=P(None, ctx, "z", None),
        check_vma=False,
    )
```

```python
import functools

import jax
import jax.numpy as jnp
from jax import lax
from jax.experimental import pallas as pl
from jax.experimental.pallas import tpu as pltpu
from jax.sharding import Mesh
from jax.sharding import PartitionSpec as P

NX, NY, NC, NZ = 4, 8, 2, 8
TOK, HD, PIECE = 256, 128, 512
D = NZ * PIECE
STEP = 0.1 * D ** (-0.5)
F32, BF16 = jnp.float32, jnp.bfloat16


def replicate(x, n):
    return jnp.broadcast_to(x[None], (n,) + x.shape)


def exchange(x, axes):
    return lax.all_to_all(x, axes, 0, 0, tiled=True)


def column_order(kinds, x_major):
    cols = kinds * 2 * HD
    row = lax.broadcasted_iota(jnp.int32, (cols, cols), 0)
    col = lax.broadcasted_iota(jnp.int32, (cols, cols), 1)
    j = row & 1
    sign = (row >> 1) & 1
    kind = (row >> 2) & (kinds - 1)
    rest = row >> (2 + (kinds - 1))
    core = rest & 1
    chip = rest >> 1
    if not x_major:
        chip = (chip & (NX - 1)) * NY + (chip >> 2)
    target = (kind * 2 + sign) * HD + (chip * 2 + core) * 2 + j
    return (col == target).astype(BF16)


def signs_and_order(acc, order):
    cols = acc.shape[1]
    lane = lax.broadcasted_iota(jnp.int32, acc.shape, 1)
    left = pltpu.roll(acc, cols - 2, 1)
    right = pltpu.roll(acc, 2, 1)
    step = jnp.float32(STEP)
    signed = jnp.where((lane & 3) < 2, acc + step * left, right + (-step) * acc).astype(BF16)
    return jnp.dot(signed, order, preferred_element_type=F32).astype(BF16)


NT = (((1,), (1,)), ((), ()))
TN = (((0,), (0,)), ((), ()))


def accumulate(own_ref, other_ref, weight_ref, acc):
    @pl.when(pl.program_id(0) == 0)
    def _():
        acc[...] = jnp.zeros_like(acc)

    weight = weight_ref[...]
    for block, ref in enumerate((own_ref, other_ref)):
        acc[block] += lax.dot_general(ref[0], weight, NT, preferred_element_type=F32)


def query_kernel(z_ref, own_ref, other_ref, weight_ref, order_ref, out_ref, acc):
    accumulate(own_ref, other_ref, weight_ref, acc)

    @pl.when(pl.program_id(0) == NZ - 1)
    def _():
        for block in range(2):
            rows = signs_and_order(acc[block], order_ref[...])
            for s in range(2):
                out_ref[block, s] = rows[:, s * HD : (s + 1) * HD]


def key_value_kernel(
    z_ref, own_ref, other_ref, weight_ref, order_ref, out_ref, state_ref, total_ref, acc
):
    accumulate(own_ref, other_ref, weight_ref, acc)

    @pl.when(pl.program_id(0) == NZ - 1)
    def _():
        for block in range(2):
            rows = signs_and_order(acc[block], order_ref[...])
            for s in range(2):
                key = rows[:, s * HD : (s + 1) * HD]
                value = rows[:, (2 + s) * HD : (3 + s) * HD]
                out_ref[0, block, s] = key
                out_ref[1, block, s] = value
                state_ref[block, s] = lax.dot_general(key, value, TN, preferred_element_type=F32)
        total_ref[...] = (state_ref[0] + state_ref[1]).astype(BF16)


def project(kernel, z, own, other, weight, order, out_shape):
    rows = weight.shape[0]
    piece = pl.BlockSpec((1, TOK, PIECE), lambda k, z: (k, 0, 0))
    whole = jax.tree.map(
        lambda s: pl.BlockSpec(s.shape, lambda k, z, n=len(s.shape): (0,) * n), out_shape
    )
    return pl.pallas_call(
        kernel,
        grid_spec=pltpu.PrefetchScalarGridSpec(
            num_scalar_prefetch=1,
            grid=(NZ,),
            in_specs=[
                piece,
                piece,
                pl.BlockSpec((rows, PIECE), lambda k, z: (0, (z[0] + k) & (NZ - 1))),
                pl.BlockSpec((rows, rows), lambda k, z: (0, 0)),
            ],
            out_specs=whole,
            scratch_shapes=[pltpu.VMEM((2, TOK, rows), F32)],
        ),
        out_shape=out_shape,
        compiler_params=pltpu.CompilerParams(
            dimension_semantics=("arbitrary",), vmem_limit_bytes=16 << 20
        ),
    )(z, own, other, pltpu.with_memory_space_constraint(weight, pltpu.HBM), order)


def inner_kernel(query_ref, kv_ref, out_ref):
    row = lax.broadcasted_iota(jnp.int32, (TOK, TOK), 0)
    col = lax.broadcasted_iota(jnp.int32, (TOK, TOK), 1)
    for block in range(2):
        for s in range(2):
            scores = lax.dot_general(
                query_ref[block, s], kv_ref[0, block, s], NT, preferred_element_type=F32
            )
            weights = jnp.where(col <= row, scores, 0.0).astype(BF16)
            out_ref[block, s] = jnp.dot(weights, kv_ref[1, block, s], preferred_element_type=F32)


def cross_kernel(query_ref, inner_ref, state_ref, partial_ref, out_ref):
    core = lax.axis_index("c")
    prior = jnp.sum(partial_ref[...].astype(F32), axis=0)
    for block in range(2):
        later = jnp.where(core == (1 - block), jnp.float32(1.0), jnp.float32(0.0))
        for s in range(2):
            carried = (prior[s] + later * state_ref[1 - block, s]).astype(BF16)
            combined = inner_ref[block, s] + jnp.dot(
                query_ref[block, s], carried, preferred_element_type=F32
            )
            scale = lax.rsqrt(jnp.mean(combined * combined, axis=-1, keepdims=True) + 1e-05)
            out_ref[block, s] = (combined * scale).astype(BF16)


def call(kernel, out_shape, *args):
    return pl.pallas_call(
        kernel,
        out_shape=out_shape,
        in_specs=[pl.BlockSpec(memory_space=pltpu.VMEM)] * len(args),
        out_specs=pl.BlockSpec(memory_space=pltpu.VMEM),
        compiler_params=pltpu.CompilerParams(vmem_limit_bytes=12 << 20),
    )(*args)


def shape(*dims, dtype=BF16):
    return jax.ShapeDtypeStruct(dims, dtype)


def token_ring(piece):
    up = [(i, (i + 1) % NZ) for i in range(NZ)]
    down = [(i, (i - 1) % NZ) for i in range(NZ)]
    below, above = [piece], [piece]
    for hop in range(NZ // 2):
        below.append(lax.ppermute(below[-1], "z", up))
        if hop < NZ // 2 - 1:
            above.append(lax.ppermute(above[-1], "z", down))
    return jnp.stack(above + below[:0:-1])


def on_device(hidden_in, proj_weights, directions):
    x, y, c, z = (lax.axis_index(name) for name in "xycz")
    swap = [(0, 1), (1, 0)]

    both = jnp.stack(
        [jnp.transpose(proj_weights, (0, 2, 3, 1)), jnp.transpose(directions, (0, 2, 3, 1))], axis=2
    )
    kv_rows = jnp.transpose(both[1:], (1, 0, 2, 3, 4)).reshape(NC, 8, D)
    q_rows = both[0].reshape(NC, 4, D)

    kv_part = exchange(replicate(kv_rows, NX).reshape(NX * NC, 8, D), ("x", "c"))
    kv_weight = lax.all_gather(kv_part.reshape(64, D), "y", axis=0, tiled=True)
    own = token_ring(hidden_in)
    other = lax.ppermute(own, "c", swap)
    q_part = exchange(replicate(q_rows, NY).reshape(NY * NC, 4, D), ("y", "c"))
    q_weight = exchange(replicate(q_part.reshape(64, D), NX), "x").reshape(256, D)

    where = z.astype(jnp.int32).reshape(1)
    query = project(
        query_kernel, where, own, other, q_weight, column_order(1, True), shape(2, 2, TOK, HD)
    )
    kv_weight, query = lax.optimization_barrier((kv_weight, query))
    kv, state, total = project(
        key_value_kernel,
        where,
        own,
        other,
        kv_weight,
        column_order(2, False),
        (shape(2, 2, 2, TOK, HD), shape(2, 2, HD, HD, dtype=F32), shape(2, HD, HD)),
    )

    over_x = exchange(replicate(total, NX), "x")
    before = (jnp.arange(NX) < x).astype(F32)
    earlier = jnp.sum(over_x.astype(F32) * before[:, None, None, None], axis=0)
    later = (jnp.arange(NY) > y).astype(F32)
    sent = earlier[None] + later[:, None, None, None] * (state[0] + state[1])[None]
    partial = exchange(sent.astype(BF16), "y")

    inner = call(inner_kernel, shape(2, 2, TOK, HD, dtype=F32), query, kv)
    out = call(cross_kernel, shape(2, 2, TOK, HD), query, inner, state, partial)
    mine, theirs = out[0], lax.ppermute(out[1], "c", swap)
    first = jnp.where(c == 0, mine, theirs)
    second = jnp.where(c == 0, theirs, mine)
    return jnp.stack([first, second], axis=2)


def solution(mesh):
    mesh4 = Mesh(mesh.devices.reshape(NX, NY, NC, NZ), ("x", "y", "c", "z"))
    ctx = ("x", "y", "c")
    return jax.shard_map(
        on_device,
        mesh=mesh4,
        in_specs=(P(ctx, "z"), P(None, None, "z", ctx), P(None, None, "z", ctx)),
        out_specs=P(None, ctx, "z", None),
        check_vma=False,
    )
```

```python
import functools

import jax
import jax.numpy as jnp
from jax import lax
from jax.experimental import pallas as pl
from jax.experimental.pallas import tpu as pltpu
from jax.sharding import Mesh
from jax.sharding import PartitionSpec as P

NX, NY, NC, NZ = 4, 8, 2, 8
TOK, HD, PIECE = 256, 128, 512
D = NZ * PIECE
STEP = 0.1 * D ** (-0.5)
F32, BF16 = jnp.float32, jnp.bfloat16


def replicate(x, n):
    return jnp.broadcast_to(x[None], (n,) + x.shape)


def exchange(x, axes):
    return lax.all_to_all(x, axes, 0, 0, tiled=True)


def column_order(kinds, first_x=None):
    cols = kinds * 2 * HD
    row = lax.broadcasted_iota(jnp.int32, (cols, cols), 0)
    col = lax.broadcasted_iota(jnp.int32, (cols, cols), 1)
    j = row & 1
    sign = (row >> 1) & 1
    kind = (row >> 2) & (kinds - 1)
    rest = row >> (2 + (kinds - 1))
    core = rest & 1
    chip = rest >> 1
    if first_x is None:
        chip = (chip & (NX - 1)) * NY + (chip >> 2)
    else:
        chip = (chip + first_x * NY) & (NX * NY - 1)
    target = (kind * 2 + sign) * HD + (chip * 2 + core) * 2 + j
    return (col == target).astype(BF16)


def signs_and_order(acc, order):
    cols = acc.shape[1]
    lane = lax.broadcasted_iota(jnp.int32, acc.shape, 1)
    left = pltpu.roll(acc, cols - 2, 1)
    right = pltpu.roll(acc, 2, 1)
    step = jnp.float32(STEP)
    signed = jnp.where((lane & 3) < 2, acc + step * left, right + (-step) * acc).astype(BF16)
    return jnp.dot(signed, order, preferred_element_type=F32).astype(BF16)


NT = (((1,), (1,)), ((), ()))
TN = (((0,), (0,)), ((), ()))


CHUNKS = 4
PER = NZ // CHUNKS


def multiply(z_ref, own_ref, other_ref, weight_hbm, weight, acc, sem):
    copies = []
    for k in range(NZ):
        start = pl.multiple_of(((z_ref[0] + k) & (NZ - 1)) * PIECE, PIECE)
        copies.append(
            pltpu.make_async_copy(
                weight_hbm.at[:, pl.ds(start, PIECE)],
                weight.at[k // PER, :, pl.ds((k % PER) * PIECE, PIECE)],
                sem.at[k],
            )
        )
    for copy in copies:
        copy.start()
    for k in range(CHUNKS):
        pieces = range(k * PER, (k + 1) * PER)
        for i in pieces:
            copies[i].wait()
        tokens = jnp.concatenate(
            [jnp.concatenate([ref[i] for i in pieces], 1) for ref in (own_ref, other_ref)], 0
        )
        part = lax.dot_general(tokens, weight[k], NT, preferred_element_type=F32)
        if k == 0:
            acc[...] = part
        else:
            acc[...] += part


def query_kernel(z_ref, own_ref, other_ref, weight_hbm, order_ref, out_ref, weight, acc, sem):
    multiply(z_ref, own_ref, other_ref, weight_hbm, weight, acc, sem)
    rows = signs_and_order(acc[...], order_ref[...])
    for block in range(2):
        for s in range(2):
            out_ref[block, s] = rows[block * TOK : (block + 1) * TOK, s * HD : (s + 1) * HD]


def key_value_kernel(
    z_ref, own_ref, other_ref, weight_hbm, order_ref, out_ref, state_ref, total_ref, weight, acc, sem
):
    multiply(z_ref, own_ref, other_ref, weight_hbm, weight, acc, sem)
    rows = signs_and_order(acc[...], order_ref[...])
    for s in range(2):
        for block in range(2):
            part = rows[block * TOK : (block + 1) * TOK]
            key = part[:, s * HD : (s + 1) * HD]
            value = part[:, (2 + s) * HD : (3 + s) * HD]
            out_ref[0, block, s] = key
            out_ref[1, block, s] = value
            state_ref[block, s] = lax.dot_general(key, value, TN, preferred_element_type=F32)
        total = (state_ref[0, s] + state_ref[1, s]).reshape(NX * NY // 2, 8, HD)
        total_ref[s * NX * NY // 2 : (s + 1) * NX * NY // 2] = total.astype(BF16)


def project(kernel, z, own, other, weight, order, out_shape):
    rows = weight.shape[0]
    vmem = pl.BlockSpec(memory_space=pltpu.VMEM)
    return pl.pallas_call(
        kernel,
        in_specs=[
            pl.BlockSpec(memory_space=pltpu.SMEM),
            vmem,
            vmem,
            pl.BlockSpec(memory_space=pltpu.HBM),
            vmem,
        ],
        out_specs=jax.tree.map(lambda s: vmem, out_shape),
        scratch_shapes=[
            pltpu.VMEM((CHUNKS, rows, PER * PIECE), BF16),
            pltpu.VMEM((2 * TOK, rows), F32),
            pltpu.SemaphoreType.DMA((NZ,)),
        ],
        out_shape=out_shape,
        compiler_params=pltpu.CompilerParams(vmem_limit_bytes=24 << 20),
    )(z, own, other, pltpu.with_memory_space_constraint(weight, pltpu.HBM), order)


def prefix_kernel(total_ref, out_ref):
    run = jnp.zeros(total_ref.shape[1:], F32)
    for chip in range(NX * NY):
        out_ref[chip] = run.astype(BF16)
        run = run + total_ref[chip].astype(F32)


def inner_kernel(query_ref, kv_ref, out_ref):
    row = lax.broadcasted_iota(jnp.int32, (TOK, TOK), 0)
    col = lax.broadcasted_iota(jnp.int32, (TOK, TOK), 1)
    for block in range(2):
        for s in range(2):
            scores = lax.dot_general(
                query_ref[block, s], kv_ref[0, block, s], NT, preferred_element_type=F32
            )
            weights = jnp.where(col <= row, scores, 0.0).astype(BF16)
            out_ref[block, s] = jnp.dot(weights, kv_ref[1, block, s], preferred_element_type=F32)


def cross_kernel(query_ref, inner_ref, state_ref, prior_ref, out_ref):
    core = lax.axis_index("c")
    prior = prior_ref[...].astype(F32).reshape(2, HD, HD)
    for block in range(2):
        later = jnp.where(core == (1 - block), jnp.float32(1.0), jnp.float32(0.0))
        for s in range(2):
            carried = (prior[s] + later * state_ref[1 - block, s]).astype(BF16)
            combined = inner_ref[block, s] + jnp.dot(
                query_ref[block, s], carried, preferred_element_type=F32
            )
            scale = lax.rsqrt(jnp.mean(combined * combined, axis=-1, keepdims=True) + 1e-05)
            out_ref[block, s] = (combined * scale).astype(BF16)


def call(kernel, out_shape, *args):
    return pl.pallas_call(
        kernel,
        out_shape=out_shape,
        in_specs=[pl.BlockSpec(memory_space=pltpu.VMEM)] * len(args),
        out_specs=pl.BlockSpec(memory_space=pltpu.VMEM),
        compiler_params=pltpu.CompilerParams(vmem_limit_bytes=12 << 20),
    )(*args)


def shape(*dims, dtype=BF16):
    return jax.ShapeDtypeStruct(dims, dtype)


def token_ring(piece):
    up = [(i, (i + 1) % NZ) for i in range(NZ)]
    down = [(i, (i - 1) % NZ) for i in range(NZ)]
    below, above = [piece], [piece]
    for hop in range(NZ // 2):
        below.append(lax.ppermute(below[-1], "z", up))
        if hop < NZ // 2 - 1:
            above.append(lax.ppermute(above[-1], "z", down))
    return jnp.stack(above + below[:0:-1])


def on_device(hidden_in, proj_weights, directions):
    x, c, z = (lax.axis_index(name) for name in "xcz")
    swap = [(0, 1), (1, 0)]

    both = jnp.stack(
        [jnp.transpose(proj_weights, (0, 2, 3, 1)), jnp.transpose(directions, (0, 2, 3, 1))], axis=2
    )
    kv_rows = jnp.transpose(both[1:], (1, 0, 2, 3, 4)).reshape(NC, 8, D)
    q_rows = both[0].reshape(NC, 4, D)

    kv_part = exchange(replicate(kv_rows, NX).reshape(NX * NC, 8, D), ("x", "c"))
    kv_weight = lax.all_gather(kv_part.reshape(64, D), "y", axis=0, tiled=True)
    own = token_ring(hidden_in)
    other = lax.ppermute(own, "c", swap)
    q_part = exchange(replicate(q_rows, NY).reshape(NY * NC, 4, D), ("y", "c"))
    q_mine = q_part.reshape(64, D)
    q_weight = jnp.concatenate(
        [q_mine] + [lax.ppermute(q_mine, "x", [(i, (i - k) % NX) for i in range(NX)]) for k in (1, 2, 3)]
    )

    where = z.astype(jnp.int32).reshape(1)
    query = project(
        query_kernel, where, own, other, q_weight, column_order(1, x), shape(2, 2, TOK, HD)
    )
    kv, state, total = project(
        key_value_kernel,
        where,
        own,
        other,
        kv_weight,
        column_order(2),
        (shape(2, 2, 2, TOK, HD), shape(2, 2, HD, HD, dtype=F32), shape(NX * NY, 8, HD)),
    )

    slices = call(prefix_kernel, shape(NX * NY, 8, HD), exchange(total, ("x", "y")))
    prior = exchange(slices, ("x", "y"))

    inner = call(inner_kernel, shape(2, 2, TOK, HD, dtype=F32), query, kv)
    out = call(cross_kernel, shape(2, 2, TOK, HD), query, inner, state, prior)
    mine, theirs = out[0], lax.ppermute(out[1], "c", swap)
    first = jnp.where(c == 0, mine, theirs)
    second = jnp.where(c == 0, theirs, mine)
    return jnp.stack([first, second], axis=2)


def solution(mesh):
    mesh4 = Mesh(mesh.devices.reshape(NX, NY, NC, NZ), ("x", "y", "c", "z"))
    ctx = ("x", "y", "c")
    return jax.shard_map(
        on_device,
        mesh=mesh4,
        in_specs=(P(ctx, "z"), P(None, None, "z", ctx), P(None, None, "z", ctx)),
        out_specs=P(None, ctx, "z", None),
        check_vma=False,
    )
```

```python
import functools

import jax
import jax.numpy as jnp
from jax import lax
from jax.experimental import pallas as pl
from jax.experimental.pallas import tpu as pltpu
from jax.sharding import Mesh
from jax.sharding import PartitionSpec as P

NX, NY, NC, NZ = 4, 8, 2, 8
TOK, HD, PIECE = 256, 128, 512
D = NZ * PIECE
STEP = 0.1 * D ** (-0.5)
F32, BF16 = jnp.float32, jnp.bfloat16


def replicate(x, n):
    return jnp.broadcast_to(x[None], (n,) + x.shape)


def exchange(x, axes):
    return lax.all_to_all(x, axes, 0, 0, tiled=True)


def column_order(kinds, first_x=None):
    cols = kinds * 2 * HD
    row = lax.broadcasted_iota(jnp.int32, (cols, cols), 0)
    col = lax.broadcasted_iota(jnp.int32, (cols, cols), 1)
    j = row & 1
    sign = (row >> 1) & 1
    kind = (row >> 2) & (kinds - 1)
    rest = row >> (2 + (kinds - 1))
    core = rest & 1
    chip = rest >> 1
    if first_x is None:
        chip = (chip & (NX - 1)) * NY + (chip >> 2)
    else:
        chip = (chip + first_x * NY) & (NX * NY - 1)
    target = (kind * 2 + sign) * HD + (chip * 2 + core) * 2 + j
    return (col == target).astype(BF16)


def signs_and_order(acc, order):
    cols = acc.shape[1]
    lane = lax.broadcasted_iota(jnp.int32, acc.shape, 1)
    left = pltpu.roll(acc, cols - 2, 1)
    right = pltpu.roll(acc, 2, 1)
    step = jnp.float32(STEP)
    signed = jnp.where((lane & 3) < 2, acc + step * left, right + (-step) * acc).astype(BF16)
    return jnp.dot(signed, order, preferred_element_type=F32).astype(BF16)


NT = (((1,), (1,)), ((), ()))
TN = (((0,), (0,)), ((), ()))


CHUNKS = 4
PER = NZ // CHUNKS


def multiply(z_ref, own_ref, other_hbm, weights_hbm, other, weight, acc, sem):
    copies = []
    for k in range(NZ):
        start = pl.multiple_of(((z_ref[0] + k) & (NZ - 1)) * PIECE, PIECE)
        columns = pl.ds((k % PER) * PIECE, PIECE)
        group = [pltpu.make_async_copy(other_hbm.at[k], other.at[k], sem.at[k, 0])]
        for i, part in enumerate(weights_hbm):
            rows = part.shape[0]
            group.append(
                pltpu.make_async_copy(
                    part.at[:, pl.ds(start, PIECE)],
                    weight.at[k // PER, pl.ds(i * rows, rows), columns],
                    sem.at[k, i + 1],
                )
            )
        for copy in group:
            copy.start()
        copies.append(group)
    for k in range(CHUNKS):
        pieces = range(k * PER, (k + 1) * PER)
        for i in pieces:
            for copy in copies[i]:
                copy.wait()
        tokens = jnp.concatenate(
            [jnp.concatenate([ref[i] for i in pieces], 1) for ref in (own_ref, other)], 0
        )
        part = lax.dot_general(tokens, weight[k], NT, preferred_element_type=F32)
        if k == 0:
            acc[...] = part
        else:
            acc[...] += part


def query_kernel(z_ref, own_ref, order_ref, other_hbm, *refs):
    weights_hbm, (out_ref, other, weight, acc, sem) = refs[:-5], refs[-5:]
    multiply(z_ref, own_ref, other_hbm, weights_hbm, other, weight, acc, sem)
    rows = signs_and_order(acc[...], order_ref[...])
    for block in range(2):
        for s in range(2):
            out_ref[block, s] = rows[block * TOK : (block + 1) * TOK, s * HD : (s + 1) * HD]


def key_value_kernel(z_ref, own_ref, order_ref, other_hbm, *refs):
    weights_hbm, (out_ref, state_ref, total_ref, other, weight, acc, sem) = refs[:-7], refs[-7:]
    multiply(z_ref, own_ref, other_hbm, weights_hbm, other, weight, acc, sem)
    rows = signs_and_order(acc[...], order_ref[...])
    for s in range(2):
        for block in range(2):
            part = rows[block * TOK : (block + 1) * TOK]
            key = part[:, s * HD : (s + 1) * HD]
            value = part[:, (2 + s) * HD : (3 + s) * HD]
            out_ref[0, block, s] = key
            out_ref[1, block, s] = value
            state_ref[block, s] = lax.dot_general(key, value, TN, preferred_element_type=F32)
        total = (state_ref[0, s] + state_ref[1, s]).reshape(NX * NY // 2, 8, HD)
        total_ref[s * NX * NY // 2 : (s + 1) * NX * NY // 2] = total.astype(BF16)


def project(kernel, z, own, other, weights, order, out_shape):
    rows = sum(weight.shape[0] for weight in weights)
    vmem = pl.BlockSpec(memory_space=pltpu.VMEM)
    far = [pltpu.with_memory_space_constraint(a, pltpu.HBM) for a in (other, *weights)]
    return pl.pallas_call(
        kernel,
        in_specs=[pl.BlockSpec(memory_space=pltpu.SMEM), vmem, vmem]
        + [pl.BlockSpec(memory_space=pltpu.HBM)] * len(far),
        out_specs=jax.tree.map(lambda s: vmem, out_shape),
        scratch_shapes=[
            pltpu.VMEM(other.shape, BF16),
            pltpu.VMEM((CHUNKS, rows, PER * PIECE), BF16),
            pltpu.VMEM((2 * TOK, rows), F32),
            pltpu.SemaphoreType.DMA((NZ, len(far))),
        ],
        out_shape=out_shape,
        compiler_params=pltpu.CompilerParams(vmem_limit_bytes=24 << 20),
    )(z, own, order, *far)


def prefix_kernel(total_ref, out_ref):
    run = jnp.zeros(total_ref.shape[1:], F32)
    for chip in range(NX * NY):
        out_ref[chip] = run.astype(BF16)
        run = run + total_ref[chip].astype(F32)


def inner_kernel(query_ref, kv_ref, out_ref):
    row = lax.broadcasted_iota(jnp.int32, (TOK, TOK), 0)
    col = lax.broadcasted_iota(jnp.int32, (TOK, TOK), 1)
    for block in range(2):
        for s in range(2):
            scores = lax.dot_general(
                query_ref[block, s], kv_ref[0, block, s], NT, preferred_element_type=F32
            )
            weights = jnp.where(col <= row, scores, 0.0).astype(BF16)
            out_ref[block, s] = jnp.dot(weights, kv_ref[1, block, s], preferred_element_type=F32)


def cross_kernel(query_ref, inner_ref, state_ref, prior_ref, out_ref):
    core = lax.axis_index("c")
    prior = prior_ref[...].astype(F32).reshape(2, HD, HD)
    for block in range(2):
        later = jnp.where(core == (1 - block), jnp.float32(1.0), jnp.float32(0.0))
        for s in range(2):
            carried = (prior[s] + later * state_ref[1 - block, s]).astype(BF16)
            combined = inner_ref[block, s] + jnp.dot(
                query_ref[block, s], carried, preferred_element_type=F32
            )
            scale = lax.rsqrt(jnp.mean(combined * combined, axis=-1, keepdims=True) + 1e-05)
            out_ref[block, s] = (combined * scale).astype(BF16)


def call(kernel, out_shape, *args):
    return pl.pallas_call(
        kernel,
        out_shape=out_shape,
        in_specs=[pl.BlockSpec(memory_space=pltpu.VMEM)] * len(args),
        out_specs=pl.BlockSpec(memory_space=pltpu.VMEM),
        compiler_params=pltpu.CompilerParams(vmem_limit_bytes=12 << 20),
    )(*args)


def shape(*dims, dtype=BF16):
    return jax.ShapeDtypeStruct(dims, dtype)


def token_ring(piece, q_part):
    up = [(i, (i + 1) % NZ) for i in range(NZ)]
    down = [(i, (i - 1) % NZ) for i in range(NZ)]
    below, above = [piece], [piece]
    for hop in range(NZ // 2):
        below.append(lax.ppermute(below[-1], "z", up))
        if hop < NZ // 2 - 1:
            above.append(lax.ppermute(above[-1], "z", down))
        if hop == 0:
            below[1], above[1], q_part = lax.optimization_barrier((below[1], above[1], q_part))
    return jnp.stack(above + below[:0:-1]), q_part


def on_device(hidden_in, proj_weights, directions):
    x, c, z = (lax.axis_index(name) for name in "xcz")
    swap = [(0, 1), (1, 0)]

    both = jnp.stack(
        [jnp.transpose(proj_weights, (0, 2, 3, 1)), jnp.transpose(directions, (0, 2, 3, 1))], axis=2
    )
    kv_rows = jnp.transpose(both[1:], (1, 0, 2, 3, 4)).reshape(NC, 8, D)
    q_rows = both[0].reshape(NC, 4, D)

    kv_part = exchange(replicate(kv_rows, NX).reshape(NX * NC, 8, D), ("x", "c"))
    kv_weight = lax.all_gather(kv_part.reshape(64, D), "y", axis=0, tiled=True)
    q_part = exchange(replicate(q_rows, NY).reshape(NY * NC, 4, D), ("y", "c"))
    own, q_part = token_ring(hidden_in, q_part)
    other = lax.ppermute(own, "c", swap)
    q_mine = q_part.reshape(64, D)
    q_weights = [q_mine] + [
        lax.ppermute(q_mine, "x", [(i, (i - k) % NX) for i in range(NX)]) for k in range(1, NX)
    ]

    where = z.astype(jnp.int32).reshape(1)
    query = project(
        query_kernel, where, own, other, q_weights, column_order(1, x), shape(2, 2, TOK, HD)
    )
    kv, state, total = project(
        key_value_kernel,
        where,
        own,
        other,
        [kv_weight],
        column_order(2),
        (shape(2, 2, 2, TOK, HD), shape(2, 2, HD, HD, dtype=F32), shape(NX * NY, 8, HD)),
    )

    slices = call(prefix_kernel, shape(NX * NY, 8, HD), exchange(total, ("x", "y")))
    prior = exchange(slices, ("x", "y"))

    inner = call(inner_kernel, shape(2, 2, TOK, HD, dtype=F32), query, kv)
    out = call(cross_kernel, shape(2, 2, TOK, HD), query, inner, state, prior)
    mine, theirs = out[0], lax.ppermute(out[1], "c", swap)
    first = jnp.where(c == 0, mine, theirs)
    second = jnp.where(c == 0, theirs, mine)
    return jnp.stack([first, second], axis=2)


def solution(mesh):
    mesh4 = Mesh(mesh.devices.reshape(NX, NY, NC, NZ), ("x", "y", "c", "z"))
    ctx = ("x", "y", "c")
    return jax.shard_map(
        on_device,
        mesh=mesh4,
        in_specs=(P(ctx, "z"), P(None, None, "z", ctx), P(None, None, "z", ctx)),
        out_specs=P(None, ctx, "z", None),
        check_vma=False,
    )
```

```python
import functools

import jax
import jax.numpy as jnp
from jax import lax
from jax.experimental import pallas as pl
from jax.experimental.pallas import tpu as pltpu
from jax.sharding import Mesh
from jax.sharding import PartitionSpec as P

NX, NY, NC, NZ = 4, 8, 2, 8
TOK, HD, PIECE = 256, 128, 512
D = NZ * PIECE
STEP = 0.1 * D ** (-0.5)
F32, BF16 = jnp.float32, jnp.bfloat16


def replicate(x, n):
    return jnp.broadcast_to(x[None], (n,) + x.shape)


def exchange(x, axes):
    return lax.all_to_all(x, axes, 0, 0, tiled=True)


def column_order(kinds, first_x=None):
    cols = kinds * 2 * HD
    row = lax.broadcasted_iota(jnp.int32, (cols, cols), 0)
    col = lax.broadcasted_iota(jnp.int32, (cols, cols), 1)
    j = row & 1
    sign = (row >> 1) & 1
    kind = (row >> 2) & (kinds - 1)
    rest = row >> (2 + (kinds - 1))
    core = rest & 1
    chip = rest >> 1
    if first_x is None:
        chip = (chip & (NX - 1)) * NY + (chip >> 2)
    else:
        chip = (chip + first_x * NY) & (NX * NY - 1)
    target = (kind * 2 + sign) * HD + (chip * 2 + core) * 2 + j
    return (col == target).astype(BF16)


def signs_and_order(acc, order):
    cols = acc.shape[1]
    lane = lax.broadcasted_iota(jnp.int32, acc.shape, 1)
    left = pltpu.roll(acc, cols - 2, 1)
    right = pltpu.roll(acc, 2, 1)
    step = jnp.float32(STEP)
    signed = jnp.where((lane & 3) < 2, acc + step * left, right + (-step) * acc).astype(BF16)
    return jnp.dot(signed, order, preferred_element_type=F32).astype(BF16)


NT = (((1,), (1,)), ((), ()))
TN = (((0,), (0,)), ((), ()))


CHUNKS = 4
PER = NZ // CHUNKS


def multiply(z_ref, own_ref, other_hbm, weights_hbm, other, weight, acc, sem):
    copies = []
    for k in range(NZ):
        start = pl.multiple_of(((z_ref[0] + k) & (NZ - 1)) * PIECE, PIECE)
        columns = pl.ds((k % PER) * PIECE, PIECE)
        group = [pltpu.make_async_copy(other_hbm.at[k], other.at[k], sem.at[k, 0])]
        for i, part in enumerate(weights_hbm):
            rows = part.shape[0]
            group.append(
                pltpu.make_async_copy(
                    part.at[:, pl.ds(start, PIECE)],
                    weight.at[k // PER, pl.ds(i * rows, rows), columns],
                    sem.at[k, i + 1],
                )
            )
        for copy in group:
            copy.start()
        copies.append(group)
    for k in range(CHUNKS):
        pieces = range(k * PER, (k + 1) * PER)
        for i in pieces:
            for copy in copies[i]:
                copy.wait()
        tokens = jnp.concatenate(
            [jnp.concatenate([ref[i] for i in pieces], 1) for ref in (own_ref, other)], 0
        )
        part = lax.dot_general(tokens, weight[k], NT, preferred_element_type=F32)
        if k == 0:
            acc[...] = part
        else:
            acc[...] += part


def query_kernel(z_ref, own_ref, order_ref, other_hbm, *refs):
    weights_hbm, (out_ref, other, weight, acc, sem) = refs[:-5], refs[-5:]
    multiply(z_ref, own_ref, other_hbm, weights_hbm, other, weight, acc, sem)
    rows = signs_and_order(acc[...], order_ref[...])
    for block in range(2):
        for s in range(2):
            out_ref[block, s] = rows[block * TOK : (block + 1) * TOK, s * HD : (s + 1) * HD]


def key_value_kernel(z_ref, own_ref, order_ref, other_hbm, *refs):
    weights_hbm, (out_ref, state_ref, total_ref, other, weight, acc, sem) = refs[:-7], refs[-7:]
    multiply(z_ref, own_ref, other_hbm, weights_hbm, other, weight, acc, sem)
    rows = signs_and_order(acc[...], order_ref[...])
    for s in range(2):
        for block in range(2):
            part = rows[block * TOK : (block + 1) * TOK]
            key = part[:, s * HD : (s + 1) * HD]
            value = part[:, (2 + s) * HD : (3 + s) * HD]
            out_ref[0, block, s] = key
            out_ref[1, block, s] = value
            state_ref[block, s] = lax.dot_general(key, value, TN, preferred_element_type=F32)
        total = (state_ref[0, s] + state_ref[1, s]).reshape(NX * NY // 2, 8, HD)
        total_ref[s * NX * NY // 2 : (s + 1) * NX * NY // 2] = total.astype(BF16)


def project(kernel, z, own, other, weights, order, out_shape):
    rows = sum(weight.shape[0] for weight in weights)
    vmem = pl.BlockSpec(memory_space=pltpu.VMEM)
    far = [pltpu.with_memory_space_constraint(a, pltpu.HBM) for a in (other, *weights)]
    return pl.pallas_call(
        kernel,
        in_specs=[pl.BlockSpec(memory_space=pltpu.SMEM), vmem, vmem]
        + [pl.BlockSpec(memory_space=pltpu.HBM)] * len(far),
        out_specs=jax.tree.map(lambda s: vmem, out_shape),
        scratch_shapes=[
            pltpu.VMEM(other.shape, BF16),
            pltpu.VMEM((CHUNKS, rows, PER * PIECE), BF16),
            pltpu.VMEM((2 * TOK, rows), F32),
            pltpu.SemaphoreType.DMA((NZ, len(far))),
        ],
        out_shape=out_shape,
        compiler_params=pltpu.CompilerParams(vmem_limit_bytes=24 << 20),
    )(z, own, order, *far)


def prefix_kernel(total_ref, out_ref):
    run = jnp.zeros(total_ref.shape[1:], F32)
    for chip in range(NX * NY):
        out_ref[chip] = run.astype(BF16)
        run = run + total_ref[chip].astype(F32)


def inner_kernel(query_ref, kv_ref, out_ref):
    row = lax.broadcasted_iota(jnp.int32, (TOK, TOK), 0)
    col = lax.broadcasted_iota(jnp.int32, (TOK, TOK), 1)
    for block in range(2):
        for s in range(2):
            scores = lax.dot_general(
                query_ref[block, s], kv_ref[0, block, s], NT, preferred_element_type=F32
            )
            weights = jnp.where(col <= row, scores, 0.0).astype(BF16)
            out_ref[block, s] = jnp.dot(weights, kv_ref[1, block, s], preferred_element_type=F32)


def cross_kernel(query_ref, inner_ref, state_ref, prior_ref, out_ref):
    core = lax.axis_index("c")
    prior = prior_ref[...].astype(F32).reshape(2, HD, HD)
    for block in range(2):
        later = jnp.where(core == (1 - block), jnp.float32(1.0), jnp.float32(0.0))
        for s in range(2):
            carried = (prior[s] + later * state_ref[1 - block, s]).astype(BF16)
            combined = inner_ref[block, s] + jnp.dot(
                query_ref[block, s], carried, preferred_element_type=F32
            )
            scale = lax.rsqrt(jnp.mean(combined * combined, axis=-1, keepdims=True) + 1e-05)
            out_ref[block, s] = (combined * scale).astype(BF16)


def call(kernel, out_shape, *args):
    return pl.pallas_call(
        kernel,
        out_shape=out_shape,
        in_specs=[pl.BlockSpec(memory_space=pltpu.VMEM)] * len(args),
        out_specs=pl.BlockSpec(memory_space=pltpu.VMEM),
        compiler_params=pltpu.CompilerParams(vmem_limit_bytes=12 << 20),
    )(*args)


def shape(*dims, dtype=BF16):
    return jax.ShapeDtypeStruct(dims, dtype)


def token_ring(piece, q_rows):
    up = [(i, (i + 1) % NZ) for i in range(NZ)]
    down = [(i, (i - 1) % NZ) for i in range(NZ)]
    below, above = [piece], [piece]
    for hop in range(NZ // 2):
        if hop == NZ // 2 - 1:
            below[hop], above[hop], q_part = lax.optimization_barrier((below[hop], above[hop], q_part))
        below.append(lax.ppermute(below[-1], "z", up))
        if hop < NZ // 2 - 1:
            above.append(lax.ppermute(above[-1], "z", down))
        if hop == 0:
            below[1], above[1], q_rows = lax.optimization_barrier((below[1], above[1], q_rows))
            q_part = exchange(replicate(q_rows, NY).reshape(NY * NC, 4, D), ("y", "c"))
    return jnp.stack(above + below[:0:-1]), q_part


def on_device(hidden_in, proj_weights, directions):
    x, c, z = (lax.axis_index(name) for name in "xcz")
    swap = [(0, 1), (1, 0)]

    both = jnp.stack(
        [jnp.transpose(proj_weights, (0, 2, 3, 1)), jnp.transpose(directions, (0, 2, 3, 1))], axis=2
    )
    kv_rows = jnp.transpose(both[1:], (1, 0, 2, 3, 4)).reshape(NC, 8, D)
    q_rows = both[0].reshape(NC, 4, D)

    kv_part = exchange(replicate(kv_rows, NX).reshape(NX * NC, 8, D), ("x", "c"))
    kv_weight = lax.all_gather(kv_part.reshape(64, D), "y", axis=0, tiled=True)
    own, q_part = token_ring(hidden_in, q_rows)
    other = lax.ppermute(own, "c", swap)
    q_mine = q_part.reshape(64, D)
    q_weights = [q_mine] + [
        lax.ppermute(q_mine, "x", [(i, (i - k) % NX) for i in range(NX)]) for k in range(1, NX)
    ]

    where = z.astype(jnp.int32).reshape(1)
    query = project(
        query_kernel, where, own, other, q_weights, column_order(1, x), shape(2, 2, TOK, HD)
    )
    kv, state, total = project(
        key_value_kernel,
        where,
        own,
        other,
        [kv_weight],
        column_order(2),
        (shape(2, 2, 2, TOK, HD), shape(2, 2, HD, HD, dtype=F32), shape(NX * NY, 8, HD)),
    )

    slices = call(prefix_kernel, shape(NX * NY, 8, HD), exchange(total, ("x", "y")))
    prior = exchange(slices, ("x", "y"))

    inner = call(inner_kernel, shape(2, 2, TOK, HD, dtype=F32), query, kv)
    out = call(cross_kernel, shape(2, 2, TOK, HD), query, inner, state, prior)
    mine, theirs = out[0], lax.ppermute(out[1], "c", swap)
    first = jnp.where(c == 0, mine, theirs)
    second = jnp.where(c == 0, theirs, mine)
    return jnp.stack([first, second], axis=2)


def solution(mesh):
    mesh4 = Mesh(mesh.devices.reshape(NX, NY, NC, NZ), ("x", "y", "c", "z"))
    ctx = ("x", "y", "c")
    return jax.shard_map(
        on_device,
        mesh=mesh4,
        in_specs=(P(ctx, "z"), P(None, None, "z", ctx), P(None, None, "z", ctx)),
        out_specs=P(None, ctx, "z", None),
        check_vma=False,
    )
```

```python
import functools

import jax
import jax.numpy as jnp
from jax import lax
from jax.experimental import pallas as pl
from jax.experimental.pallas import tpu as pltpu
from jax.sharding import Mesh
from jax.sharding import PartitionSpec as P

NX, NY, NC, NZ = 4, 8, 2, 8
TOK, HD, PIECE = 256, 128, 512
D = NZ * PIECE
STEP = 0.1 * D ** (-0.5)
F32, BF16 = jnp.float32, jnp.bfloat16


def replicate(x, n):
    return jnp.broadcast_to(x[None], (n,) + x.shape)


def exchange(x, axes):
    return lax.all_to_all(x, axes, 0, 0, tiled=True)


def column_order(kinds, first_x=None, first_core=None):
    cols = kinds * 2 * HD
    row = lax.broadcasted_iota(jnp.int32, (cols, cols), 0)
    col = lax.broadcasted_iota(jnp.int32, (cols, cols), 1)
    j = row & 1
    sign = (row >> 1) & 1
    kind = (row >> 2) & (kinds - 1)
    rest = row >> (2 + (kinds - 1))
    core = rest & 1
    chip = rest >> 1
    if first_x is None:
        chip = (chip & (NX - 1)) * NY + (chip >> 2)
    else:
        chip = (chip + first_x * NY) & (NX * NY - 1)
        core = core ^ first_core
    target = (kind * 2 + sign) * HD + (chip * 2 + core) * 2 + j
    return (col == target).astype(BF16)


def signs_and_order(acc, order):
    cols = acc.shape[1]
    lane = lax.broadcasted_iota(jnp.int32, acc.shape, 1)
    left = pltpu.roll(acc, cols - 2, 1)
    right = pltpu.roll(acc, 2, 1)
    step = jnp.float32(STEP)
    signed = jnp.where((lane & 3) < 2, acc + step * left, right + (-step) * acc).astype(BF16)
    return jnp.dot(signed, order, preferred_element_type=F32).astype(BF16)


NT = (((1,), (1,)), ((), ()))
TN = (((0,), (0,)), ((), ()))


CHUNKS = 4
PER = NZ // CHUNKS


def multiply(own_ref, other_hbm, weights_hbm, other, weight, acc, sem):
    copies = []
    for k in range(NZ):
        columns = pl.ds((k % PER) * PIECE, PIECE)
        group = [pltpu.make_async_copy(other_hbm.at[k], other.at[k], sem.at[k, 0])]
        for i, part in enumerate(weights_hbm):
            rows = part.shape[0]
            group.append(
                pltpu.make_async_copy(
                    part.at[:, pl.ds(k * PIECE, PIECE)],
                    weight.at[k // PER, pl.ds(i * rows, rows), columns],
                    sem.at[k, i + 1],
                )
            )
        for copy in group:
            copy.start()
        copies.append(group)
    for k in range(CHUNKS):
        pieces = range(k * PER, (k + 1) * PER)
        for i in pieces:
            for copy in copies[i]:
                copy.wait()
        tokens = jnp.concatenate(
            [jnp.concatenate([ref[i] for i in pieces], 1) for ref in (own_ref, other)], 0
        )
        part = lax.dot_general(tokens, weight[k], NT, preferred_element_type=F32)
        if k == 0:
            acc[...] = part
        else:
            acc[...] += part


def query_kernel(own_ref, order_ref, other_hbm, *refs):
    weights_hbm, (out_ref, other, weight, acc, sem) = refs[:-5], refs[-5:]
    multiply(own_ref, other_hbm, weights_hbm, other, weight, acc, sem)
    rows = signs_and_order(acc[...], order_ref[...])
    for block in range(2):
        for s in range(2):
            out_ref[block, s] = rows[block * TOK : (block + 1) * TOK, s * HD : (s + 1) * HD]


def key_value_kernel(own_ref, order_ref, other_hbm, *refs):
    weights_hbm, (out_ref, state_ref, total_ref, other, weight, acc, sem) = refs[:-7], refs[-7:]
    multiply(own_ref, other_hbm, weights_hbm, other, weight, acc, sem)
    rows = signs_and_order(acc[...], order_ref[...])
    for s in range(2):
        for block in range(2):
            part = rows[block * TOK : (block + 1) * TOK]
            key = part[:, s * HD : (s + 1) * HD]
            value = part[:, (2 + s) * HD : (3 + s) * HD]
            out_ref[0, block, s] = key
            out_ref[1, block, s] = value
            state_ref[block, s] = lax.dot_general(key, value, TN, preferred_element_type=F32)
        total = (state_ref[0, s] + state_ref[1, s]).reshape(NX * NY // 2, 8, HD)
        total_ref[s * NX * NY // 2 : (s + 1) * NX * NY // 2] = total.astype(BF16)


def project(kernel, own, other, weights, order, out_shape):
    rows = sum(weight.shape[0] for weight in weights)
    vmem = pl.BlockSpec(memory_space=pltpu.VMEM)
    far = [pltpu.with_memory_space_constraint(a, pltpu.HBM) for a in (other, *weights)]
    return pl.pallas_call(
        kernel,
        in_specs=[vmem, vmem]
        + [pl.BlockSpec(memory_space=pltpu.HBM)] * len(far),
        out_specs=jax.tree.map(lambda s: vmem, out_shape),
        scratch_shapes=[
            pltpu.VMEM(other.shape, BF16),
            pltpu.VMEM((CHUNKS, rows, PER * PIECE), BF16),
            pltpu.VMEM((2 * TOK, rows), F32),
            pltpu.SemaphoreType.DMA((NZ, len(far))),
        ],
        out_shape=out_shape,
        compiler_params=pltpu.CompilerParams(vmem_limit_bytes=24 << 20),
    )(own, order, *far)


def prefix_kernel(total_ref, out_ref):
    run = jnp.zeros(total_ref.shape[1:], F32)
    for chip in range(NX * NY):
        out_ref[chip] = run.astype(BF16)
        run = run + total_ref[chip].astype(F32)


def inner_kernel(query_ref, kv_ref, out_ref):
    row = lax.broadcasted_iota(jnp.int32, (TOK, TOK), 0)
    col = lax.broadcasted_iota(jnp.int32, (TOK, TOK), 1)
    for block in range(2):
        for s in range(2):
            scores = lax.dot_general(
                query_ref[block, s], kv_ref[0, block, s], NT, preferred_element_type=F32
            )
            weights = jnp.where(col <= row, scores, 0.0).astype(BF16)
            out_ref[block, s] = jnp.dot(weights, kv_ref[1, block, s], preferred_element_type=F32)


def cross_kernel(query_ref, inner_ref, state_ref, prior_ref, out_ref):
    core = lax.axis_index("c")
    prior = prior_ref[...].astype(F32).reshape(2, HD, HD)
    for block in range(2):
        later = jnp.where(core == (1 - block), jnp.float32(1.0), jnp.float32(0.0))
        for s in range(2):
            carried = (prior[s] + later * state_ref[1 - block, s]).astype(BF16)
            combined = inner_ref[block, s] + jnp.dot(
                query_ref[block, s], carried, preferred_element_type=F32
            )
            scale = lax.rsqrt(jnp.mean(combined * combined, axis=-1, keepdims=True) + 1e-05)
            out_ref[block, s] = (combined * scale).astype(BF16)


def call(kernel, out_shape, *args):
    return pl.pallas_call(
        kernel,
        out_shape=out_shape,
        in_specs=[pl.BlockSpec(memory_space=pltpu.VMEM)] * len(args),
        out_specs=pl.BlockSpec(memory_space=pltpu.VMEM),
        compiler_params=pltpu.CompilerParams(vmem_limit_bytes=12 << 20),
    )(*args)


def shape(*dims, dtype=BF16):
    return jax.ShapeDtypeStruct(dims, dtype)


def on_device(hidden_in, proj_weights, directions):
    x, c = lax.axis_index("x"), lax.axis_index("c")
    swap = [(0, 1), (1, 0)]

    both = jnp.stack(
        [jnp.transpose(proj_weights, (0, 2, 3, 1)), jnp.transpose(directions, (0, 2, 3, 1))], axis=2
    )
    kv_rows = jnp.transpose(both[1:], (1, 0, 2, 3, 4)).reshape(NC, 8, D)
    q_rows = both[0].reshape(NC, 4, D)

    kv_part = exchange(replicate(kv_rows, NX).reshape(NX * NC, 8, D), ("x", "c"))
    kv_weight = lax.all_gather(kv_part.reshape(64, D), "y", axis=0, tiled=True)
    own = exchange(replicate(hidden_in, NZ), "z")

    q_first, q_second = q_rows[0], q_rows[1]
    q_mine = jnp.where(c == 0, q_first, q_second)
    q_theirs = lax.ppermute(jnp.where(c == 0, q_second, q_first), "c", swap)
    q_part = lax.all_gather(jnp.concatenate([q_mine, q_theirs]), "y", axis=0, tiled=True)
    q_weights = [q_part] + [
        lax.ppermute(q_part, "x", [(i, (i - k) % NX) for i in range(NX)]) for k in range(1, NX)
    ]
    own, q_weights = lax.optimization_barrier((own, q_weights))
    other = lax.ppermute(own, "c", swap)

    query = project(
        query_kernel, own, other, q_weights, column_order(1, x, c), shape(2, 2, TOK, HD)
    )
    kv, state, total = project(
        key_value_kernel,
        own,
        other,
        [kv_weight],
        column_order(2),
        (shape(2, 2, 2, TOK, HD), shape(2, 2, HD, HD, dtype=F32), shape(NX * NY, 8, HD)),
    )

    slices = call(prefix_kernel, shape(NX * NY, 8, HD), exchange(total, ("x", "y")))
    prior = exchange(slices, ("x", "y"))

    inner = call(inner_kernel, shape(2, 2, TOK, HD, dtype=F32), query, kv)
    out = call(cross_kernel, shape(2, 2, TOK, HD), query, inner, state, prior)
    mine, theirs = out[0], lax.ppermute(out[1], "c", swap)
    first = jnp.where(c == 0, mine, theirs)
    second = jnp.where(c == 0, theirs, mine)
    return jnp.stack([first, second], axis=2)


def solution(mesh):
    mesh4 = Mesh(mesh.devices.reshape(NX, NY, NC, NZ), ("x", "y", "c", "z"))
    ctx = ("x", "y", "c")
    return jax.shard_map(
        on_device,
        mesh=mesh4,
        in_specs=(P(ctx, "z"), P(None, None, "z", ctx), P(None, None, "z", ctx)),
        out_specs=P(None, ctx, "z", None),
        check_vma=False,
    )
```

```python
import functools

import jax
import jax.numpy as jnp
from jax import lax
from jax.experimental import pallas as pl
from jax.experimental.pallas import tpu as pltpu
from jax.sharding import Mesh
from jax.sharding import PartitionSpec as P

NX, NY, NC, NZ = 4, 8, 2, 8
TOK, HD, PIECE = 256, 128, 512
D = NZ * PIECE
STEP = 0.1 * D ** (-0.5)
F32, BF16 = jnp.float32, jnp.bfloat16


def replicate(x, n):
    return jnp.broadcast_to(x[None], (n,) + x.shape)


def exchange(x, axes):
    return lax.all_to_all(x, axes, 0, 0, tiled=True)


def column_order(kinds, first_x=None, first_core=None):
    cols = kinds * 2 * HD
    row = lax.broadcasted_iota(jnp.int32, (cols, cols), 0)
    col = lax.broadcasted_iota(jnp.int32, (cols, cols), 1)
    j = row & 1
    sign = (row >> 1) & 1
    kind = (row >> 2) & (kinds - 1)
    rest = row >> (2 + (kinds - 1))
    core = rest & 1
    chip = rest >> 1
    if first_x is None:
        chip = (chip & (NX - 1)) * NY + (chip >> 2)
    else:
        chip = (chip + first_x * NY) & (NX * NY - 1)
        core = core ^ first_core
    target = (kind * 2 + sign) * HD + (chip * 2 + core) * 2 + j
    return (col == target).astype(BF16)


def signs_and_order(acc, order):
    cols = acc.shape[1]
    lane = lax.broadcasted_iota(jnp.int32, acc.shape, 1)
    left = pltpu.roll(acc, cols - 2, 1)
    right = pltpu.roll(acc, 2, 1)
    step = jnp.float32(STEP)
    signed = jnp.where((lane & 3) < 2, acc + step * left, right + (-step) * acc).astype(BF16)
    return jnp.dot(signed, order, preferred_element_type=F32).astype(BF16)


NT = (((1,), (1,)), ((), ()))
TN = (((0,), (0,)), ((), ()))


CHUNKS = 4
PER = NZ // CHUNKS


def multiply(own_ref, other_hbm, weights_hbm, other, weight, acc, sem):
    copies = []
    for k in range(NZ):
        columns = pl.ds((k % PER) * PIECE, PIECE)
        group = [pltpu.make_async_copy(other_hbm.at[k], other.at[k], sem.at[k, 0])]
        first = 0
        for i, part in enumerate(weights_hbm):
            rows = part.shape[0]
            group.append(
                pltpu.make_async_copy(
                    part.at[:, pl.ds(k * PIECE, PIECE)],
                    weight.at[k // PER, pl.ds(first, rows), columns],
                    sem.at[k, i + 1],
                )
            )
            first += rows
        for copy in group:
            copy.start()
        copies.append(group)
    for k in range(CHUNKS):
        pieces = range(k * PER, (k + 1) * PER)
        for i in pieces:
            for copy in copies[i]:
                copy.wait()
        tokens = jnp.concatenate(
            [jnp.concatenate([ref[i] for i in pieces], 1) for ref in (own_ref, other)], 0
        )
        part = lax.dot_general(tokens, weight[k], NT, preferred_element_type=F32)
        if k == 0:
            acc[...] = part
        else:
            acc[...] += part


def query_kernel(own_ref, order_ref, other_hbm, *refs):
    weights_hbm, (out_ref, other, weight, acc, sem) = refs[:-5], refs[-5:]
    multiply(own_ref, other_hbm, weights_hbm, other, weight, acc, sem)
    rows = signs_and_order(acc[...], order_ref[...])
    for block in range(2):
        for s in range(2):
            out_ref[block, s] = rows[block * TOK : (block + 1) * TOK, s * HD : (s + 1) * HD]


def key_value_kernel(own_ref, order_ref, other_hbm, *refs):
    weights_hbm, (out_ref, state_ref, total_ref, other, weight, acc, sem) = refs[:-7], refs[-7:]
    multiply(own_ref, other_hbm, weights_hbm, other, weight, acc, sem)
    rows = signs_and_order(acc[...], order_ref[...])
    for s in range(2):
        for block in range(2):
            part = rows[block * TOK : (block + 1) * TOK]
            key = part[:, s * HD : (s + 1) * HD]
            value = part[:, (2 + s) * HD : (3 + s) * HD]
            out_ref[0, block, s] = key
            out_ref[1, block, s] = value
            state_ref[block, s] = lax.dot_general(key, value, TN, preferred_element_type=F32)
        total = (state_ref[0, s] + state_ref[1, s]).reshape(NX * NY // 2, 8, HD)
        total_ref[s * NX * NY // 2 : (s + 1) * NX * NY // 2] = total.astype(BF16)


def project(kernel, own, other, weights, order, out_shape):
    rows = sum(weight.shape[0] for weight in weights)
    vmem = pl.BlockSpec(memory_space=pltpu.VMEM)
    far = [pltpu.with_memory_space_constraint(a, pltpu.HBM) for a in (other, *weights)]
    return pl.pallas_call(
        kernel,
        in_specs=[vmem, vmem]
        + [pl.BlockSpec(memory_space=pltpu.HBM)] * len(far),
        out_specs=jax.tree.map(lambda s: vmem, out_shape),
        scratch_shapes=[
            pltpu.VMEM(other.shape, BF16),
            pltpu.VMEM((CHUNKS, rows, PER * PIECE), BF16),
            pltpu.VMEM((2 * TOK, rows), F32),
            pltpu.SemaphoreType.DMA((NZ, len(far))),
        ],
        out_shape=out_shape,
        compiler_params=pltpu.CompilerParams(vmem_limit_bytes=24 << 20),
    )(own, order, *far)


def prefix_kernel(total_ref, out_ref):
    run = jnp.zeros(total_ref.shape[1:], F32)
    for chip in range(NX * NY):
        out_ref[chip] = run.astype(BF16)
        run = run + total_ref[chip].astype(F32)


def inner_kernel(query_ref, kv_ref, out_ref):
    row = lax.broadcasted_iota(jnp.int32, (TOK, TOK), 0)
    col = lax.broadcasted_iota(jnp.int32, (TOK, TOK), 1)
    for block in range(2):
        for s in range(2):
            scores = lax.dot_general(
                query_ref[block, s], kv_ref[0, block, s], NT, preferred_element_type=F32
            )
            weights = jnp.where(col <= row, scores, 0.0).astype(BF16)
            out_ref[block, s] = jnp.dot(weights, kv_ref[1, block, s], preferred_element_type=F32)


def cross_kernel(query_ref, inner_ref, state_ref, prior_ref, out_ref):
    core = lax.axis_index("c")
    prior = prior_ref[...].astype(F32).reshape(2, HD, HD)
    for block in range(2):
        later = jnp.where(core == (1 - block), jnp.float32(1.0), jnp.float32(0.0))
        for s in range(2):
            carried = (prior[s] + later * state_ref[1 - block, s]).astype(BF16)
            combined = inner_ref[block, s] + jnp.dot(
                query_ref[block, s], carried, preferred_element_type=F32
            )
            scale = lax.rsqrt(jnp.mean(combined * combined, axis=-1, keepdims=True) + 1e-05)
            out_ref[block, s] = (combined * scale).astype(BF16)


def call(kernel, out_shape, *args):
    return pl.pallas_call(
        kernel,
        out_shape=out_shape,
        in_specs=[pl.BlockSpec(memory_space=pltpu.VMEM)] * len(args),
        out_specs=pl.BlockSpec(memory_space=pltpu.VMEM),
        compiler_params=pltpu.CompilerParams(vmem_limit_bytes=12 << 20),
    )(*args)


def shape(*dims, dtype=BF16):
    return jax.ShapeDtypeStruct(dims, dtype)


def on_device(hidden_in, proj_weights, directions):
    x, c = lax.axis_index("x"), lax.axis_index("c")
    swap = [(0, 1), (1, 0)]

    both = jnp.stack(
        [jnp.transpose(proj_weights, (0, 2, 3, 1)), jnp.transpose(directions, (0, 2, 3, 1))], axis=2
    )
    kv_rows = jnp.transpose(both[1:], (1, 0, 2, 3, 4)).reshape(NC, 8, D)
    q_rows = both[0].reshape(NC, 4, D)

    kv_part = exchange(replicate(kv_rows, NX).reshape(NX * NC, 8, D), ("x", "c"))
    kv_weight = lax.all_gather(kv_part.reshape(64, D), "y", axis=0, tiled=True)
    own = exchange(replicate(hidden_in, NZ), "z")

    q_first, q_second = q_rows[0], q_rows[1]
    q_mine = jnp.where(c == 0, q_first, q_second)
    q_theirs = lax.ppermute(jnp.where(c == 0, q_second, q_first), "c", swap)
    q_part = lax.all_gather(jnp.concatenate([q_mine, q_theirs]), "y", axis=0, tiled=True)
    up = [(i, (i + 1) % NX) for i in range(NX)]
    down = [(i, (i - 1) % NX) for i in range(NX)]
    q_after, q_before = lax.ppermute(q_part, "x", down), lax.ppermute(q_part, "x", up)
    own, q_after, q_before = lax.optimization_barrier((own, q_after, q_before))
    other = lax.ppermute(own, "c", swap)
    half = q_part.shape[0] // 2
    q_far = [lax.ppermute(q_after[:half], "x", down), lax.ppermute(q_before[half:], "x", up)]
    q_weights = [q_part, q_after, *q_far, q_before]

    query = project(
        query_kernel, own, other, q_weights, column_order(1, x, c), shape(2, 2, TOK, HD)
    )
    kv, state, total = project(
        key_value_kernel,
        own,
        other,
        [kv_weight],
        column_order(2),
        (shape(2, 2, 2, TOK, HD), shape(2, 2, HD, HD, dtype=F32), shape(NX * NY, 8, HD)),
    )

    slices = call(prefix_kernel, shape(NX * NY, 8, HD), exchange(total, ("x", "y")))
    prior = exchange(slices, ("x", "y"))

    inner = call(inner_kernel, shape(2, 2, TOK, HD, dtype=F32), query, kv)
    out = call(cross_kernel, shape(2, 2, TOK, HD), query, inner, state, prior)
    mine, theirs = out[0], lax.ppermute(out[1], "c", swap)
    first = jnp.where(c == 0, mine, theirs)
    second = jnp.where(c == 0, theirs, mine)
    return jnp.stack([first, second], axis=2)


def solution(mesh):
    mesh4 = Mesh(mesh.devices.reshape(NX, NY, NC, NZ), ("x", "y", "c", "z"))
    ctx = ("x", "y", "c")
    return jax.shard_map(
        on_device,
        mesh=mesh4,
        in_specs=(P(ctx, "z"), P(None, None, "z", ctx), P(None, None, "z", ctx)),
        out_specs=P(None, ctx, "z", None),
        check_vma=False,
    )
```

```python
import functools

import jax
import jax.numpy as jnp
from jax import lax
from jax.experimental import pallas as pl
from jax.experimental.pallas import tpu as pltpu
from jax.sharding import Mesh
from jax.sharding import PartitionSpec as P

NX, NY, NC, NZ = 4, 8, 2, 8
TOK, HD, PIECE = 256, 128, 512
D = NZ * PIECE
STEP = 0.1 * D ** (-0.5)
F32, BF16 = jnp.float32, jnp.bfloat16


def replicate(x, n):
    return jnp.broadcast_to(x[None], (n,) + x.shape)


def exchange(x, axes):
    return lax.all_to_all(x, axes, 0, 0, tiled=True)


def column_order(kinds, first_x=None, first_core=None):
    cols = kinds * 2 * HD
    row = lax.broadcasted_iota(jnp.int32, (cols, cols), 0)
    col = lax.broadcasted_iota(jnp.int32, (cols, cols), 1)
    j = row & 1
    sign = (row >> 1) & 1
    kind = (row >> 2) & (kinds - 1)
    rest = row >> (2 + (kinds - 1))
    core = rest & 1
    chip = rest >> 1
    if first_x is None:
        chip = (chip & (NX - 1)) * NY + (chip >> 2)
    else:
        chip = (chip + first_x * NY) & (NX * NY - 1)
        core = core ^ first_core
    target = (kind * 2 + sign) * HD + (chip * 2 + core) * 2 + j
    return (col == target).astype(BF16)


def signs_and_order(acc, order):
    cols = acc.shape[1]
    lane = lax.broadcasted_iota(jnp.int32, acc.shape, 1)
    left = pltpu.roll(acc, cols - 2, 1)
    right = pltpu.roll(acc, 2, 1)
    step = jnp.float32(STEP)
    signed = jnp.where((lane & 3) < 2, acc + step * left, right + (-step) * acc).astype(BF16)
    return jnp.dot(signed, order, preferred_element_type=F32).astype(BF16)


NT = (((1,), (1,)), ((), ()))
TN = (((0,), (0,)), ((), ()))


CHUNKS = 4
PER = NZ // CHUNKS


def multiply(own_ref, other_hbm, weights_hbm, other, weight, acc, sem):
    copies = []
    for k in range(NZ):
        columns = pl.ds((k % PER) * PIECE, PIECE)
        group = [pltpu.make_async_copy(other_hbm.at[k], other.at[k], sem.at[k, 0])]
        first = 0
        for i, part in enumerate(weights_hbm):
            rows = part.shape[0]
            group.append(
                pltpu.make_async_copy(
                    part.at[:, pl.ds(k * PIECE, PIECE)],
                    weight.at[k // PER, pl.ds(first, rows), columns],
                    sem.at[k, i + 1],
                )
            )
            first += rows
        for copy in group:
            copy.start()
        copies.append(group)
    for k in range(CHUNKS):
        pieces = range(k * PER, (k + 1) * PER)
        for i in pieces:
            for copy in copies[i]:
                copy.wait()
        tokens = jnp.concatenate(
            [jnp.concatenate([ref[i] for i in pieces], 1) for ref in (own_ref, other)], 0
        )
        part = lax.dot_general(tokens, weight[k], NT, preferred_element_type=F32)
        if k == 0:
            acc[...] = part
        else:
            acc[...] += part


def query_kernel(own_ref, order_ref, other_hbm, *refs):
    weights_hbm, (out_ref, other, weight, acc, sem) = refs[:-5], refs[-5:]
    multiply(own_ref, other_hbm, weights_hbm, other, weight, acc, sem)
    rows = signs_and_order(acc[...], order_ref[...])
    for block in range(2):
        for s in range(2):
            out_ref[block, s] = rows[block * TOK : (block + 1) * TOK, s * HD : (s + 1) * HD]


def key_value_kernel(own_ref, order_ref, other_hbm, *refs):
    weights_hbm, (out_ref, state_ref, total_ref, other, weight, acc, sem) = refs[:-7], refs[-7:]
    multiply(own_ref, other_hbm, weights_hbm, other, weight, acc, sem)
    rows = signs_and_order(acc[...], order_ref[...])
    for s in range(2):
        for block in range(2):
            part = rows[block * TOK : (block + 1) * TOK]
            key = part[:, s * HD : (s + 1) * HD]
            value = part[:, (2 + s) * HD : (3 + s) * HD]
            out_ref[0, block, s] = key
            out_ref[1, block, s] = value
            state_ref[block, s] = lax.dot_general(key, value, TN, preferred_element_type=F32)
        total = (state_ref[0, s] + state_ref[1, s]).reshape(NX * NY // 2, 8, HD)
        total_ref[s * NX * NY // 2 : (s + 1) * NX * NY // 2] = total.astype(BF16)


def project(kernel, own, other, weights, order, out_shape):
    rows = sum(weight.shape[0] for weight in weights)
    vmem = pl.BlockSpec(memory_space=pltpu.VMEM)
    far = [pltpu.with_memory_space_constraint(a, pltpu.HBM) for a in (other, *weights)]
    return pl.pallas_call(
        kernel,
        in_specs=[vmem, vmem]
        + [pl.BlockSpec(memory_space=pltpu.HBM)] * len(far),
        out_specs=jax.tree.map(lambda s: vmem, out_shape),
        scratch_shapes=[
            pltpu.VMEM(other.shape, BF16),
            pltpu.VMEM((CHUNKS, rows, PER * PIECE), BF16),
            pltpu.VMEM((2 * TOK, rows), F32),
            pltpu.SemaphoreType.DMA((NZ, len(far))),
        ],
        out_shape=out_shape,
        compiler_params=pltpu.CompilerParams(vmem_limit_bytes=24 << 20),
    )(own, order, *far)


def prefix_kernel(total_ref, out_ref):
    run = jnp.zeros(total_ref.shape[1:], F32)
    for chip in range(NX * NY):
        out_ref[chip] = run.astype(BF16)
        run = run + total_ref[chip].astype(F32)


def inner_kernel(query_ref, kv_ref, out_ref):
    row = lax.broadcasted_iota(jnp.int32, (TOK, TOK), 0)
    col = lax.broadcasted_iota(jnp.int32, (TOK, TOK), 1)
    for block in range(2):
        for s in range(2):
            scores = lax.dot_general(
                query_ref[block, s], kv_ref[0, block, s], NT, preferred_element_type=F32
            )
            weights = jnp.where(col <= row, scores, 0.0).astype(BF16)
            out_ref[block, s] = jnp.dot(weights, kv_ref[1, block, s], preferred_element_type=F32)


def cross_kernel(query_ref, inner_ref, state_ref, prior_ref, out_ref):
    core = lax.axis_index("c")
    prior = prior_ref[...].astype(F32).reshape(2, HD, HD)
    for block in range(2):
        later = jnp.where(core == (1 - block), jnp.float32(1.0), jnp.float32(0.0))
        for s in range(2):
            carried = (prior[s] + later * state_ref[1 - block, s]).astype(BF16)
            combined = inner_ref[block, s] + jnp.dot(
                query_ref[block, s], carried, preferred_element_type=F32
            )
            scale = lax.rsqrt(jnp.mean(combined * combined, axis=-1, keepdims=True) + 1e-05)
            out_ref[block, s] = (combined * scale).astype(BF16)


def call(kernel, out_shape, *args):
    return pl.pallas_call(
        kernel,
        out_shape=out_shape,
        in_specs=[pl.BlockSpec(memory_space=pltpu.VMEM)] * len(args),
        out_specs=pl.BlockSpec(memory_space=pltpu.VMEM),
        compiler_params=pltpu.CompilerParams(vmem_limit_bytes=12 << 20),
    )(*args)


def shape(*dims, dtype=BF16):
    return jax.ShapeDtypeStruct(dims, dtype)


def on_device(hidden_in, proj_weights, directions):
    x, c = lax.axis_index("x"), lax.axis_index("c")
    swap = [(0, 1), (1, 0)]

    both = jnp.stack(
        [jnp.transpose(proj_weights, (0, 2, 3, 1)), jnp.transpose(directions, (0, 2, 3, 1))], axis=2
    )
    kv_rows = jnp.transpose(both[1:], (1, 0, 2, 3, 4)).reshape(NC, 8, D)
    q_rows = both[0].reshape(NC, 4, D)

    kv_part = exchange(replicate(kv_rows, NX).reshape(NX * NC, 8, D), ("x", "c"))
    kv_weight = lax.all_gather(kv_part.reshape(64, D), "y", axis=0, tiled=True)
    own = exchange(replicate(hidden_in, NZ), "z")

    q_first, q_second = q_rows[0], q_rows[1]
    q_mine = jnp.where(c == 0, q_first, q_second)
    q_theirs = lax.ppermute(jnp.where(c == 0, q_second, q_first), "c", swap)
    q_part = lax.all_gather(jnp.concatenate([q_mine, q_theirs]), "y", axis=0, tiled=True)
    up = [(i, (i + 1) % NX) for i in range(NX)]
    down = [(i, (i - 1) % NX) for i in range(NX)]
    q_after, q_before = lax.ppermute(q_part, "x", down), lax.ppermute(q_part, "x", up)
    own, q_after, q_before = lax.optimization_barrier((own, q_after, q_before))
    other = lax.ppermute(own, "c", swap)
    q_weights = [q_part, q_after, lax.ppermute(q_after, "x", down), q_before]

    query = project(
        query_kernel, own, other, q_weights, column_order(1, x, c), shape(2, 2, TOK, HD)
    )
    kv, state, total = project(
        key_value_kernel,
        own,
        other,
        [kv_weight],
        column_order(2),
        (shape(2, 2, 2, TOK, HD), shape(2, 2, HD, HD, dtype=F32), shape(NX * NY, 8, HD)),
    )

    totals, query = lax.optimization_barrier((exchange(total, ("x", "y")), query))
    slices = call(prefix_kernel, shape(NX * NY, 8, HD), totals)
    prior = exchange(slices, ("x", "y"))

    inner = call(inner_kernel, shape(2, 2, TOK, HD, dtype=F32), query, kv)
    out = call(cross_kernel, shape(2, 2, TOK, HD), query, inner, state, prior)
    mine, theirs = out[0], lax.ppermute(out[1], "c", swap)
    first = jnp.where(c == 0, mine, theirs)
    second = jnp.where(c == 0, theirs, mine)
    return jnp.stack([first, second], axis=2)


def solution(mesh):
    mesh4 = Mesh(mesh.devices.reshape(NX, NY, NC, NZ), ("x", "y", "c", "z"))
    ctx = ("x", "y", "c")
    return jax.shard_map(
        on_device,
        mesh=mesh4,
        in_specs=(P(ctx, "z"), P(None, None, "z", ctx), P(None, None, "z", ctx)),
        out_specs=P(None, ctx, "z", None),
        check_vma=False,
    )
```

```python
import functools

import jax
import jax.numpy as jnp
from jax import lax
from jax.experimental import pallas as pl
from jax.experimental.pallas import tpu as pltpu
from jax.sharding import Mesh
from jax.sharding import PartitionSpec as P

NX, NY, NC, NZ = 4, 8, 2, 8
TOK, HD, PIECE = 256, 128, 512
D = NZ * PIECE
STEP = 0.1 * D ** (-0.5)
F32, BF16 = jnp.float32, jnp.bfloat16


def replicate(x, n):
    return jnp.broadcast_to(x[None], (n,) + x.shape)


def exchange(x, axes):
    return lax.all_to_all(x, axes, 0, 0, tiled=True)


def column_order(kinds, first_x=None, first_core=None):
    cols = kinds * 2 * HD
    row = lax.broadcasted_iota(jnp.int32, (cols, cols), 0)
    col = lax.broadcasted_iota(jnp.int32, (cols, cols), 1)
    j = row & 1
    sign = (row >> 1) & 1
    kind = (row >> 2) & (kinds - 1)
    rest = row >> (2 + (kinds - 1))
    core = rest & 1
    chip = rest >> 1
    if first_x is None:
        chip = (chip & (NX - 1)) * NY + (chip >> 2)
    else:
        chip = (chip + first_x * NY) & (NX * NY - 1)
        core = core ^ first_core
    target = (kind * 2 + sign) * HD + (chip * 2 + core) * 2 + j
    return (col == target).astype(BF16)


def signs_and_order(acc, order):
    cols = acc.shape[1]
    lane = lax.broadcasted_iota(jnp.int32, acc.shape, 1)
    left = pltpu.roll(acc, cols - 2, 1)
    right = pltpu.roll(acc, 2, 1)
    step = jnp.float32(STEP)
    signed = jnp.where((lane & 3) < 2, acc + step * left, right + (-step) * acc).astype(BF16)
    return jnp.dot(signed, order, preferred_element_type=F32).astype(BF16)


NT = (((1,), (1,)), ((), ()))
TN = (((0,), (0,)), ((), ()))


CHUNKS = 4
PER = NZ // CHUNKS


def multiply(own_ref, other_hbm, weights_hbm, other, weight, acc, sem):
    copies = []
    for k in range(NZ):
        columns = pl.ds((k % PER) * PIECE, PIECE)
        group = [pltpu.make_async_copy(other_hbm.at[k], other.at[k], sem.at[k, 0])]
        first = 0
        for i, part in enumerate(weights_hbm):
            rows = part.shape[0]
            group.append(
                pltpu.make_async_copy(
                    part.at[:, pl.ds(k * PIECE, PIECE)],
                    weight.at[k // PER, pl.ds(first, rows), columns],
                    sem.at[k, i + 1],
                )
            )
            first += rows
        for copy in group:
            copy.start()
        copies.append(group)
    for k in range(CHUNKS):
        pieces = range(k * PER, (k + 1) * PER)
        for i in pieces:
            for copy in copies[i]:
                copy.wait()
        tokens = jnp.concatenate(
            [jnp.concatenate([ref[i] for i in pieces], 1) for ref in (own_ref, other)], 0
        )
        part = lax.dot_general(tokens, weight[k], NT, preferred_element_type=F32)
        if k == 0:
            acc[...] = part
        else:
            acc[...] += part


def query_kernel(own_ref, order_ref, other_hbm, *refs):
    weights_hbm, (out_ref, other, weight, acc, sem) = refs[:-5], refs[-5:]
    multiply(own_ref, other_hbm, weights_hbm, other, weight, acc, sem)
    rows = signs_and_order(acc[...], order_ref[...])
    for block in range(2):
        for s in range(2):
            out_ref[block, s] = rows[block * TOK : (block + 1) * TOK, s * HD : (s + 1) * HD]


def key_value_kernel(own_ref, order_ref, other_hbm, *refs):
    weights_hbm, (out_ref, state_ref, total_ref, other, weight, acc, sem) = refs[:-7], refs[-7:]
    multiply(own_ref, other_hbm, weights_hbm, other, weight, acc, sem)
    rows = signs_and_order(acc[...], order_ref[...])
    for s in range(2):
        for block in range(2):
            part = rows[block * TOK : (block + 1) * TOK]
            key = part[:, s * HD : (s + 1) * HD]
            value = part[:, (2 + s) * HD : (3 + s) * HD]
            out_ref[0, block, s] = key
            out_ref[1, block, s] = value
            state_ref[block, s] = lax.dot_general(key, value, TN, preferred_element_type=F32)
        total = (state_ref[0, s] + state_ref[1, s]).reshape(NX * NY // 2, 8, HD)
        total_ref[s * NX * NY // 2 : (s + 1) * NX * NY // 2] = total.astype(BF16)


def project(kernel, own, other, weights, order, out_shape):
    rows = sum(weight.shape[0] for weight in weights)
    vmem = pl.BlockSpec(memory_space=pltpu.VMEM)
    far = [pltpu.with_memory_space_constraint(a, pltpu.HBM) for a in (other, *weights)]
    return pl.pallas_call(
        kernel,
        in_specs=[vmem, vmem]
        + [pl.BlockSpec(memory_space=pltpu.HBM)] * len(far),
        out_specs=jax.tree.map(lambda s: vmem, out_shape),
        scratch_shapes=[
            pltpu.VMEM(other.shape, BF16),
            pltpu.VMEM((CHUNKS, rows, PER * PIECE), BF16),
            pltpu.VMEM((2 * TOK, rows), F32),
            pltpu.SemaphoreType.DMA((NZ, len(far))),
        ],
        out_shape=out_shape,
        compiler_params=pltpu.CompilerParams(vmem_limit_bytes=24 << 20),
    )(own, order, *far)


def arrived_kernel(block_hbm, out_ref, sem):
    copy = pltpu.make_async_copy(block_hbm.at[pl.ds(0, 8), pl.ds(0, HD)], out_ref, sem)
    copy.start()
    copy.wait()


def arrived(block):
    return pl.pallas_call(
        arrived_kernel,
        in_specs=[pl.BlockSpec(memory_space=pltpu.HBM)],
        out_specs=pl.BlockSpec(memory_space=pltpu.VMEM),
        out_shape=shape(8, HD),
        scratch_shapes=[pltpu.SemaphoreType.DMA],
    )(pltpu.with_memory_space_constraint(block, pltpu.HBM))


def prefix_kernel(total_ref, arrived_ref, out_ref):
    run = jnp.zeros(total_ref.shape[1:], F32)
    for chip in range(NX * NY):
        out_ref[chip] = run.astype(BF16)
        run = run + total_ref[chip].astype(F32)


def inner_kernel(query_ref, kv_ref, out_ref):
    row = lax.broadcasted_iota(jnp.int32, (TOK, TOK), 0)
    col = lax.broadcasted_iota(jnp.int32, (TOK, TOK), 1)
    for block in range(2):
        for s in range(2):
            scores = lax.dot_general(
                query_ref[block, s], kv_ref[0, block, s], NT, preferred_element_type=F32
            )
            weights = jnp.where(col <= row, scores, 0.0).astype(BF16)
            out_ref[block, s] = jnp.dot(weights, kv_ref[1, block, s], preferred_element_type=F32)


def cross_kernel(query_ref, inner_ref, state_ref, prior_ref, out_ref):
    core = lax.axis_index("c")
    prior = prior_ref[...].astype(F32).reshape(2, HD, HD)
    for block in range(2):
        later = jnp.where(core == (1 - block), jnp.float32(1.0), jnp.float32(0.0))
        for s in range(2):
            carried = (prior[s] + later * state_ref[1 - block, s]).astype(BF16)
            combined = inner_ref[block, s] + jnp.dot(
                query_ref[block, s], carried, preferred_element_type=F32
            )
            scale = lax.rsqrt(jnp.mean(combined * combined, axis=-1, keepdims=True) + 1e-05)
            out_ref[block, s] = (combined * scale).astype(BF16)


def call(kernel, out_shape, *args, unread=0):
    spaces = [pltpu.VMEM] * (len(args) - unread) + [pl.ANY] * unread
    return pl.pallas_call(
        kernel,
        out_shape=out_shape,
        in_specs=[pl.BlockSpec(memory_space=space) for space in spaces],
        out_specs=pl.BlockSpec(memory_space=pltpu.VMEM),
        compiler_params=pltpu.CompilerParams(vmem_limit_bytes=12 << 20),
    )(*args)


def shape(*dims, dtype=BF16):
    return jax.ShapeDtypeStruct(dims, dtype)


def on_device(hidden_in, proj_weights, directions):
    x, c = lax.axis_index("x"), lax.axis_index("c")
    swap = [(0, 1), (1, 0)]

    both = jnp.stack(
        [jnp.transpose(proj_weights, (0, 2, 3, 1)), jnp.transpose(directions, (0, 2, 3, 1))], axis=2
    )
    kv_rows = jnp.transpose(both[1:], (1, 0, 2, 3, 4)).reshape(NC, 8, D)
    q_rows = both[0].reshape(NC, 4, D)

    kv_part = exchange(replicate(kv_rows, NX).reshape(NX * NC, 8, D), ("x", "c"))
    kv_weight = lax.all_gather(kv_part.reshape(64, D), "y", axis=0, tiled=True)
    own = exchange(replicate(hidden_in, NZ), "z")

    q_first, q_second = q_rows[0], q_rows[1]
    q_mine = jnp.where(c == 0, q_first, q_second)
    q_theirs = lax.ppermute(jnp.where(c == 0, q_second, q_first), "c", swap)
    q_part = lax.all_gather(jnp.concatenate([q_mine, q_theirs]), "y", axis=0, tiled=True)
    up = [(i, (i + 1) % NX) for i in range(NX)]
    down = [(i, (i - 1) % NX) for i in range(NX)]
    q_after, q_before = lax.ppermute(q_part, "x", down), lax.ppermute(q_part, "x", up)
    own, q_after, q_before = lax.optimization_barrier((own, q_after, q_before))
    other = lax.ppermute(own, "c", swap)
    q_far = lax.ppermute(q_after, "x", down)
    q_weights = [q_part, q_after, q_far, q_before]

    query = project(
        query_kernel, own, other, q_weights, column_order(1, x, c), shape(2, 2, TOK, HD)
    )
    kv, state, total = project(
        key_value_kernel,
        own,
        other,
        [kv_weight],
        column_order(2),
        (shape(2, 2, 2, TOK, HD), shape(2, 2, HD, HD, dtype=F32), shape(NX * NY, 8, HD)),
    )

    slices = call(
        prefix_kernel, shape(NX * NY, 8, HD), exchange(total, ("x", "y")), arrived(q_far), unread=1
    )
    prior = exchange(slices, ("x", "y"))

    inner = call(inner_kernel, shape(2, 2, TOK, HD, dtype=F32), query, kv)
    out = call(cross_kernel, shape(2, 2, TOK, HD), query, inner, state, prior)
    mine, theirs = out[0], lax.ppermute(out[1], "c", swap)
    first = jnp.where(c == 0, mine, theirs)
    second = jnp.where(c == 0, theirs, mine)
    return jnp.stack([first, second], axis=2)


def solution(mesh):
    mesh4 = Mesh(mesh.devices.reshape(NX, NY, NC, NZ), ("x", "y", "c", "z"))
    ctx = ("x", "y", "c")
    return jax.shard_map(
        on_device,
        mesh=mesh4,
        in_specs=(P(ctx, "z"), P(None, None, "z", ctx), P(None, None, "z", ctx)),
        out_specs=P(None, ctx, "z", None),
        check_vma=False,
    )
```

```python
import functools

import jax
import jax.numpy as jnp
from jax import lax
from jax.experimental import pallas as pl
from jax.experimental.pallas import tpu as pltpu
from jax.sharding import Mesh
from jax.sharding import PartitionSpec as P

NX, NY, NC, NZ = 4, 8, 2, 8
TOK, HD, PIECE = 256, 128, 512
D = NZ * PIECE
STEP = 0.1 * D ** (-0.5)
F32, BF16 = jnp.float32, jnp.bfloat16


def replicate(x, n):
    return jnp.broadcast_to(x[None], (n,) + x.shape)


def exchange(x, axes):
    return lax.all_to_all(x, axes, 0, 0, tiled=True)


def column_order(kinds, first_x=None, first_core=None):
    cols = kinds * 2 * HD
    row = lax.broadcasted_iota(jnp.int32, (cols, cols), 0)
    col = lax.broadcasted_iota(jnp.int32, (cols, cols), 1)
    j = row & 1
    sign = (row >> 1) & 1
    kind = (row >> 2) & (kinds - 1)
    rest = row >> (2 + (kinds - 1))
    core = rest & 1
    chip = rest >> 1
    if first_x is None:
        chip = (chip & (NX - 1)) * NY + (chip >> 2)
    else:
        chip = (chip + first_x * NY) & (NX * NY - 1)
        core = core ^ first_core
    target = (kind * 2 + sign) * HD + (chip * 2 + core) * 2 + j
    return (col == target).astype(BF16)


def signs_and_order(acc, order):
    cols = acc.shape[1]
    lane = lax.broadcasted_iota(jnp.int32, acc.shape, 1)
    left = pltpu.roll(acc, cols - 2, 1)
    right = pltpu.roll(acc, 2, 1)
    step = jnp.float32(STEP)
    signed = jnp.where((lane & 3) < 2, acc + step * left, right + (-step) * acc).astype(BF16)
    return jnp.dot(signed, order, preferred_element_type=F32).astype(BF16)


NT = (((1,), (1,)), ((), ()))
TN = (((0,), (0,)), ((), ()))


CHUNKS = 4
PER = NZ // CHUNKS


def multiply(own_ref, other_hbm, weights_hbm, other, weight, acc, sem):
    copies = []
    for k in range(NZ):
        columns = pl.ds((k % PER) * PIECE, PIECE)
        group = [pltpu.make_async_copy(other_hbm.at[k], other.at[k], sem.at[k, 0])]
        first = 0
        for i, part in enumerate(weights_hbm):
            rows = part.shape[0]
            group.append(
                pltpu.make_async_copy(
                    part.at[:, pl.ds(k * PIECE, PIECE)],
                    weight.at[k // PER, pl.ds(first, rows), columns],
                    sem.at[k, i + 1],
                )
            )
            first += rows
        for copy in group:
            copy.start()
        copies.append(group)
    for k in range(CHUNKS):
        pieces = range(k * PER, (k + 1) * PER)
        for i in pieces:
            for copy in copies[i]:
                copy.wait()
        tokens = jnp.concatenate(
            [jnp.concatenate([ref[i] for i in pieces], 1) for ref in (own_ref, other)], 0
        )
        part = lax.dot_general(tokens, weight[k], NT, preferred_element_type=F32)
        if k == 0:
            acc[...] = part
        else:
            acc[...] += part


def query_kernel(own_ref, order_ref, other_hbm, *refs):
    weights_hbm, (out_ref, other, weight, acc, sem) = refs[:-5], refs[-5:]
    multiply(own_ref, other_hbm, weights_hbm, other, weight, acc, sem)
    rows = signs_and_order(acc[...], order_ref[...])
    for block in range(2):
        for s in range(2):
            out_ref[block, s] = rows[block * TOK : (block + 1) * TOK, s * HD : (s + 1) * HD]


def key_value_kernel(own_ref, order_ref, other_hbm, *refs):
    weights_hbm, (out_ref, state_ref, total_ref, other, weight, acc, sem) = refs[:-7], refs[-7:]
    multiply(own_ref, other_hbm, weights_hbm, other, weight, acc, sem)
    rows = signs_and_order(acc[...], order_ref[...])
    for s in range(2):
        for block in range(2):
            part = rows[block * TOK : (block + 1) * TOK]
            key = part[:, s * HD : (s + 1) * HD]
            value = part[:, (2 + s) * HD : (3 + s) * HD]
            out_ref[0, block, s] = key
            out_ref[1, block, s] = value
            state_ref[block, s] = lax.dot_general(key, value, TN, preferred_element_type=F32)
        total = (state_ref[0, s] + state_ref[1, s]).reshape(NX * NY // 2, 8, HD)
        total_ref[s * NX * NY // 2 : (s + 1) * NX * NY // 2] = total.astype(BF16)


def project(kernel, own, other, weights, order, out_shape):
    rows = sum(weight.shape[0] for weight in weights)
    vmem = pl.BlockSpec(memory_space=pltpu.VMEM)
    far = [pltpu.with_memory_space_constraint(a, pltpu.HBM) for a in (other, *weights)]
    return pl.pallas_call(
        kernel,
        in_specs=[vmem, vmem]
        + [pl.BlockSpec(memory_space=pltpu.HBM)] * len(far),
        out_specs=jax.tree.map(lambda s: vmem, out_shape),
        scratch_shapes=[
            pltpu.VMEM(other.shape, BF16),
            pltpu.VMEM((CHUNKS, rows, PER * PIECE), BF16),
            pltpu.VMEM((2 * TOK, rows), F32),
            pltpu.SemaphoreType.DMA((NZ, len(far))),
        ],
        out_shape=out_shape,
        compiler_params=pltpu.CompilerParams(vmem_limit_bytes=24 << 20),
    )(own, order, *far)


def arrived_kernel(block_hbm, out_ref, sem):
    copy = pltpu.make_async_copy(block_hbm.at[pl.ds(0, 8), pl.ds(0, HD)], out_ref, sem)
    copy.start()
    copy.wait()


def arrived(block):
    return pl.pallas_call(
        arrived_kernel,
        in_specs=[pl.BlockSpec(memory_space=pltpu.HBM)],
        out_specs=pl.BlockSpec(memory_space=pltpu.VMEM),
        out_shape=shape(8, HD),
        scratch_shapes=[pltpu.SemaphoreType.DMA],
    )(pltpu.with_memory_space_constraint(block, pltpu.HBM))


def prefix_kernel(total_ref, arrived_ref, out_ref):
    run = jnp.zeros(total_ref.shape[1:], F32)
    for chip in range(NX * NY):
        out_ref[chip] = run.astype(BF16)
        run = run + total_ref[chip].astype(F32)


def inner_kernel(query_ref, kv_ref, out_ref):
    row = lax.broadcasted_iota(jnp.int32, (TOK, TOK), 0)
    col = lax.broadcasted_iota(jnp.int32, (TOK, TOK), 1)
    for block in range(2):
        for s in range(2):
            scores = lax.dot_general(
                query_ref[block, s], kv_ref[0, block, s], NT, preferred_element_type=F32
            )
            weights = jnp.where(col <= row, scores, 0.0).astype(BF16)
            out_ref[block, s] = jnp.dot(weights, kv_ref[1, block, s], preferred_element_type=F32)


def cross_kernel(query_ref, inner_ref, state_ref, prior_ref, out_ref):
    core = lax.axis_index("c")
    prior = prior_ref[...].astype(F32).reshape(2, HD, HD)
    for block in range(2):
        later = jnp.where(core == (1 - block), jnp.float32(1.0), jnp.float32(0.0))
        for s in range(2):
            carried = (prior[s] + later * state_ref[1 - block, s]).astype(BF16)
            combined = inner_ref[block, s] + jnp.dot(
                query_ref[block, s], carried, preferred_element_type=F32
            )
            scale = lax.rsqrt(jnp.mean(combined * combined, axis=-1, keepdims=True) + 1e-05)
            out_ref[block, s] = (combined * scale).astype(BF16)


def call(kernel, out_shape, *args, unread=0):
    spaces = [pltpu.VMEM] * (len(args) - unread) + [pltpu.HBM] * unread
    args = [
        pltpu.with_memory_space_constraint(arg, space) if space is pltpu.HBM else arg
        for arg, space in zip(args, spaces)
    ]
    return pl.pallas_call(
        kernel,
        out_shape=out_shape,
        in_specs=[pl.BlockSpec(memory_space=space) for space in spaces],
        out_specs=pl.BlockSpec(memory_space=pltpu.VMEM),
        compiler_params=pltpu.CompilerParams(vmem_limit_bytes=12 << 20),
    )(*args)


def shape(*dims, dtype=BF16):
    return jax.ShapeDtypeStruct(dims, dtype)


def on_device(hidden_in, proj_weights, directions):
    x, c = lax.axis_index("x"), lax.axis_index("c")
    swap = [(0, 1), (1, 0)]

    both = jnp.stack(
        [jnp.transpose(proj_weights, (0, 2, 3, 1)), jnp.transpose(directions, (0, 2, 3, 1))], axis=2
    )
    kv_rows = jnp.transpose(both[1:], (1, 0, 2, 3, 4)).reshape(NC, 8, D)
    q_rows = both[0].reshape(NC, 4, D)

    kv_part = exchange(replicate(kv_rows, NX).reshape(NX * NC, 8, D), ("x", "c"))
    kv_weight = lax.all_gather(kv_part.reshape(64, D), "y", axis=0, tiled=True)
    own = exchange(replicate(hidden_in, NZ), "z")

    q_first, q_second = q_rows[0], q_rows[1]
    q_mine = jnp.where(c == 0, q_first, q_second)
    q_theirs = lax.ppermute(jnp.where(c == 0, q_second, q_first), "c", swap)
    q_part = lax.all_gather(jnp.concatenate([q_mine, q_theirs]), "y", axis=0, tiled=True)
    up = [(i, (i + 1) % NX) for i in range(NX)]
    down = [(i, (i - 1) % NX) for i in range(NX)]
    q_after, q_before = lax.ppermute(q_part, "x", down), lax.ppermute(q_part, "x", up)
    own, q_after, q_before = lax.optimization_barrier((own, q_after, q_before))
    other = lax.ppermute(own, "c", swap)
    q_far = lax.ppermute(q_after, "x", down)
    q_weights = [q_part, q_after, q_far, q_before]

    query = project(
        query_kernel, own, other, q_weights, column_order(1, x, c), shape(2, 2, TOK, HD)
    )
    kv, state, total = project(
        key_value_kernel,
        own,
        other,
        [kv_weight],
        column_order(2),
        (shape(2, 2, 2, TOK, HD), shape(2, 2, HD, HD, dtype=F32), shape(NX * NY, 8, HD)),
    )

    slices = call(
        prefix_kernel, shape(NX * NY, 8, HD), exchange(total, ("x", "y")), arrived(q_far), unread=1
    )
    prior = exchange(slices, ("x", "y"))

    inner = call(inner_kernel, shape(2, 2, TOK, HD, dtype=F32), query, kv)
    out = call(cross_kernel, shape(2, 2, TOK, HD), query, inner, state, prior)
    mine, theirs = out[0], lax.ppermute(out[1], "c", swap)
    first = jnp.where(c == 0, mine, theirs)
    second = jnp.where(c == 0, theirs, mine)
    return jnp.stack([first, second], axis=2)


def solution(mesh):
    mesh4 = Mesh(mesh.devices.reshape(NX, NY, NC, NZ), ("x", "y", "c", "z"))
    ctx = ("x", "y", "c")
    return jax.shard_map(
        on_device,
        mesh=mesh4,
        in_specs=(P(ctx, "z"), P(None, None, "z", ctx), P(None, None, "z", ctx)),
        out_specs=P(None, ctx, "z", None),
        check_vma=False,
    )
```

```python
import functools

import jax
import jax.numpy as jnp
from jax import lax
from jax.experimental import pallas as pl
from jax.experimental.pallas import tpu as pltpu
from jax.sharding import Mesh
from jax.sharding import PartitionSpec as P

NX, NY, NC, NZ = 4, 8, 2, 8
TOK, HD, PIECE = 256, 128, 512
D = NZ * PIECE
STEP = 0.1 * D ** (-0.5)
F32, BF16 = jnp.float32, jnp.bfloat16


def replicate(x, n):
    return jnp.broadcast_to(x[None], (n,) + x.shape)


def exchange(x, axes):
    return lax.all_to_all(x, axes, 0, 0, tiled=True)


def column_order(kinds, first_x=None, first_core=None):
    cols = kinds * 2 * HD
    row = lax.broadcasted_iota(jnp.int32, (cols, cols), 0)
    col = lax.broadcasted_iota(jnp.int32, (cols, cols), 1)
    j = row & 1
    sign = (row >> 1) & 1
    kind = (row >> 2) & (kinds - 1)
    rest = row >> (2 + (kinds - 1))
    core = rest & 1
    chip = rest >> 1
    if first_x is None:
        chip = (chip & (NX - 1)) * NY + (chip >> 2)
    else:
        chip = (chip + first_x * NY) & (NX * NY - 1)
        core = core ^ first_core
    target = (kind * 2 + sign) * HD + (chip * 2 + core) * 2 + j
    return (col == target).astype(BF16)


def signs_and_order(acc, order):
    cols = acc.shape[1]
    lane = lax.broadcasted_iota(jnp.int32, acc.shape, 1)
    left = pltpu.roll(acc, cols - 2, 1)
    right = pltpu.roll(acc, 2, 1)
    step = jnp.float32(STEP)
    signed = jnp.where((lane & 3) < 2, acc + step * left, right + (-step) * acc).astype(BF16)
    return jnp.dot(signed, order, preferred_element_type=F32).astype(BF16)


NT = (((1,), (1,)), ((), ()))
TN = (((0,), (0,)), ((), ()))


CHUNKS = 4
PER = NZ // CHUNKS


def multiply(own_ref, other_hbm, weights_hbm, other, weight, acc, sem):
    copies = []
    for k in range(NZ):
        columns = pl.ds((k % PER) * PIECE, PIECE)
        group = [pltpu.make_async_copy(other_hbm.at[k], other.at[k], sem.at[k, 0])]
        first = 0
        for i, part in enumerate(weights_hbm):
            rows = part.shape[0]
            group.append(
                pltpu.make_async_copy(
                    part.at[:, pl.ds(k * PIECE, PIECE)],
                    weight.at[k // PER, pl.ds(first, rows), columns],
                    sem.at[k, i + 1],
                )
            )
            first += rows
        for copy in group:
            copy.start()
        copies.append(group)
    for k in range(CHUNKS):
        pieces = range(k * PER, (k + 1) * PER)
        for i in pieces:
            for copy in copies[i]:
                copy.wait()
        for block, ref in enumerate((own_ref, other)):
            part = None
            for i in pieces:
                one = lax.dot_general(
                    ref[i], weight[k, :, (i % PER) * PIECE : (i % PER + 1) * PIECE], NT,
                    preferred_element_type=F32,
                )
                part = one if part is None else part + one
            if k == 0:
                acc[block * TOK : (block + 1) * TOK] = part
            else:
                acc[block * TOK : (block + 1) * TOK] += part


def query_kernel(own_ref, order_ref, other_hbm, *refs):
    weights_hbm, (out_ref, other, weight, acc, sem) = refs[:-5], refs[-5:]
    multiply(own_ref, other_hbm, weights_hbm, other, weight, acc, sem)
    rows = signs_and_order(acc[...], order_ref[...])
    for block in range(2):
        for s in range(2):
            out_ref[block, s] = rows[block * TOK : (block + 1) * TOK, s * HD : (s + 1) * HD]


def key_value_kernel(own_ref, order_ref, other_hbm, *refs):
    weights_hbm, (out_ref, state_ref, total_ref, other, weight, acc, sem) = refs[:-7], refs[-7:]
    multiply(own_ref, other_hbm, weights_hbm, other, weight, acc, sem)
    rows = signs_and_order(acc[...], order_ref[...])
    for s in range(2):
        for block in range(2):
            part = rows[block * TOK : (block + 1) * TOK]
            key = part[:, s * HD : (s + 1) * HD]
            value = part[:, (2 + s) * HD : (3 + s) * HD]
            out_ref[0, block, s] = key
            out_ref[1, block, s] = value
            state_ref[block, s] = lax.dot_general(key, value, TN, preferred_element_type=F32)
        total = (state_ref[0, s] + state_ref[1, s]).reshape(NX * NY // 2, 8, HD)
        total_ref[s * NX * NY // 2 : (s + 1) * NX * NY // 2] = total.astype(BF16)


def project(kernel, own, other, weights, order, out_shape):
    rows = sum(weight.shape[0] for weight in weights)
    vmem = pl.BlockSpec(memory_space=pltpu.VMEM)
    far = [pltpu.with_memory_space_constraint(a, pltpu.HBM) for a in (other, *weights)]
    return pl.pallas_call(
        kernel,
        in_specs=[vmem, vmem]
        + [pl.BlockSpec(memory_space=pltpu.HBM)] * len(far),
        out_specs=jax.tree.map(lambda s: vmem, out_shape),
        scratch_shapes=[
            pltpu.VMEM(other.shape, BF16),
            pltpu.VMEM((CHUNKS, rows, PER * PIECE), BF16),
            pltpu.VMEM((2 * TOK, rows), F32),
            pltpu.SemaphoreType.DMA((NZ, len(far))),
        ],
        out_shape=out_shape,
        compiler_params=pltpu.CompilerParams(vmem_limit_bytes=24 << 20),
    )(own, order, *far)


def arrived_kernel(block_hbm, out_ref, sem):
    copy = pltpu.make_async_copy(block_hbm.at[pl.ds(0, 8), pl.ds(0, HD)], out_ref, sem)
    copy.start()
    copy.wait()


def arrived(block):
    return pl.pallas_call(
        arrived_kernel,
        in_specs=[pl.BlockSpec(memory_space=pltpu.HBM)],
        out_specs=pl.BlockSpec(memory_space=pltpu.VMEM),
        out_shape=shape(8, HD),
        scratch_shapes=[pltpu.SemaphoreType.DMA],
    )(pltpu.with_memory_space_constraint(block, pltpu.HBM))


def prefix_kernel(total_ref, arrived_ref, out_ref):
    run = jnp.zeros(total_ref.shape[1:], F32)
    for chip in range(NX * NY):
        out_ref[chip] = run.astype(BF16)
        run = run + total_ref[chip].astype(F32)


def inner_kernel(query_ref, kv_ref, out_ref):
    row = lax.broadcasted_iota(jnp.int32, (TOK, TOK), 0)
    col = lax.broadcasted_iota(jnp.int32, (TOK, TOK), 1)
    for block in range(2):
        for s in range(2):
            scores = lax.dot_general(
                query_ref[block, s], kv_ref[0, block, s], NT, preferred_element_type=F32
            )
            weights = jnp.where(col <= row, scores, 0.0).astype(BF16)
            out_ref[block, s] = jnp.dot(weights, kv_ref[1, block, s], preferred_element_type=F32)


def cross_kernel(query_ref, inner_ref, state_ref, prior_ref, mine_ref, theirs_ref):
    core = lax.axis_index("c")
    prior = prior_ref[...].astype(F32).reshape(2, HD, HD)
    for block, out_ref in enumerate((mine_ref, theirs_ref)):
        later = jnp.where(core == (1 - block), jnp.float32(1.0), jnp.float32(0.0))
        for s in range(2):
            carried = (prior[s] + later * state_ref[1 - block, s]).astype(BF16)
            combined = inner_ref[block, s] + jnp.dot(
                query_ref[block, s], carried, preferred_element_type=F32
            )
            scale = lax.rsqrt(jnp.mean(combined * combined, axis=-1, keepdims=True) + 1e-05)
            out_ref[s] = (combined * scale).astype(BF16)


def call(kernel, out_shape, *args, unread=0):
    spaces = [pltpu.VMEM] * (len(args) - unread) + [pltpu.HBM] * unread
    args = [
        pltpu.with_memory_space_constraint(arg, space) if space is pltpu.HBM else arg
        for arg, space in zip(args, spaces)
    ]
    return pl.pallas_call(
        kernel,
        out_shape=out_shape,
        in_specs=[pl.BlockSpec(memory_space=space) for space in spaces],
        out_specs=jax.tree.map(lambda s: pl.BlockSpec(memory_space=pltpu.VMEM), out_shape),
        compiler_params=pltpu.CompilerParams(vmem_limit_bytes=12 << 20),
    )(*args)


def shape(*dims, dtype=BF16):
    return jax.ShapeDtypeStruct(dims, dtype)


def on_device(hidden_in, proj_weights, directions):
    x, c = lax.axis_index("x"), lax.axis_index("c")
    swap = [(0, 1), (1, 0)]

    both = jnp.stack(
        [jnp.transpose(proj_weights, (0, 2, 3, 1)), jnp.transpose(directions, (0, 2, 3, 1))], axis=2
    )
    kv_rows = jnp.transpose(both[1:], (1, 0, 2, 3, 4)).reshape(NC, 8, D)
    q_rows = both[0].reshape(NC, 4, D)

    kv_part = exchange(replicate(kv_rows, NX).reshape(NX * NC, 8, D), ("x", "c"))
    kv_weight = lax.all_gather(kv_part.reshape(64, D), "y", axis=0, tiled=True)
    own = exchange(replicate(hidden_in, NZ), "z")

    q_first, q_second = q_rows[0], q_rows[1]
    q_mine = jnp.where(c == 0, q_first, q_second)
    q_theirs = lax.ppermute(jnp.where(c == 0, q_second, q_first), "c", swap)
    q_part = lax.all_gather(jnp.concatenate([q_mine, q_theirs]), "y", axis=0, tiled=True)
    up = [(i, (i + 1) % NX) for i in range(NX)]
    down = [(i, (i - 1) % NX) for i in range(NX)]
    q_after, q_before = lax.ppermute(q_part, "x", down), lax.ppermute(q_part, "x", up)
    own, q_after, q_before = lax.optimization_barrier((own, q_after, q_before))
    other = lax.ppermute(own, "c", swap)
    q_far = lax.ppermute(q_after, "x", down)
    q_weights = [q_part, q_after, q_far, q_before]

    query = project(
        query_kernel, own, other, q_weights, column_order(1, x, c), shape(2, 2, TOK, HD)
    )
    kv, state, total = project(
        key_value_kernel,
        own,
        other,
        [kv_weight],
        column_order(2),
        (shape(2, 2, 2, TOK, HD), shape(2, 2, HD, HD, dtype=F32), shape(NX * NY, 8, HD)),
    )

    slices = call(
        prefix_kernel, shape(NX * NY, 8, HD), exchange(total, ("x", "y")), arrived(q_far), unread=1
    )
    prior = exchange(slices, ("x", "y"))

    inner = call(inner_kernel, shape(2, 2, TOK, HD, dtype=F32), query, kv)
    block = shape(2, TOK, HD)
    mine, sent = call(cross_kernel, (block, block), query, inner, state, prior)
    theirs = lax.ppermute(sent, "c", swap)
    first = jnp.where(c == 0, mine, theirs)
    second = jnp.where(c == 0, theirs, mine)
    return jnp.stack([first, second], axis=2)


def solution(mesh):
    mesh4 = Mesh(mesh.devices.reshape(NX, NY, NC, NZ), ("x", "y", "c", "z"))
    ctx = ("x", "y", "c")
    return jax.shard_map(
        on_device,
        mesh=mesh4,
        in_specs=(P(ctx, "z"), P(None, None, "z", ctx), P(None, None, "z", ctx)),
        out_specs=P(None, ctx, "z", None),
        check_vma=False,
    )
```

```python
import functools

import jax
import jax.numpy as jnp
from jax import lax
from jax.experimental import pallas as pl
from jax.experimental.pallas import tpu as pltpu
from jax.sharding import Mesh
from jax.sharding import PartitionSpec as P

NX, NY, NC, NZ = 4, 8, 2, 8
TOK, HD, PIECE = 256, 128, 512
D = NZ * PIECE
STEP = 0.1 * D ** (-0.5)
F32, BF16 = jnp.float32, jnp.bfloat16


def replicate(x, n):
    return jnp.broadcast_to(x[None], (n,) + x.shape)


def exchange(x, axes):
    return lax.all_to_all(x, axes, 0, 0, tiled=True)


def column_order(kinds, first_x=None, first_core=None):
    cols = kinds * 2 * HD
    row = lax.broadcasted_iota(jnp.int32, (cols, cols), 0)
    col = lax.broadcasted_iota(jnp.int32, (cols, cols), 1)
    j = row & 1
    sign = (row >> 1) & 1
    kind = (row >> 2) & (kinds - 1)
    rest = row >> (2 + (kinds - 1))
    core = rest & 1
    chip = rest >> 1
    if first_x is None:
        chip = (chip & (NX - 1)) * NY + (chip >> 2)
    else:
        chip = (chip + first_x * NY) & (NX * NY - 1)
        core = core ^ first_core
    target = (kind * 2 + sign) * HD + (chip * 2 + core) * 2 + j
    return (col == target).astype(BF16)


def signs_and_order(acc, order):
    cols = acc.shape[1]
    lane = lax.broadcasted_iota(jnp.int32, acc.shape, 1)
    left = pltpu.roll(acc, cols - 2, 1)
    right = pltpu.roll(acc, 2, 1)
    step = jnp.float32(STEP)
    signed = jnp.where((lane & 3) < 2, acc + step * left, right + (-step) * acc).astype(BF16)
    return jnp.dot(signed, order, preferred_element_type=F32).astype(BF16)


NT = (((1,), (1,)), ((), ()))
TN = (((0,), (0,)), ((), ()))


CHUNKS = 4
PER = NZ // CHUNKS


def multiply(own_ref, other_hbm, weights_hbm, other, weight, acc, sem):
    copies = []
    for k in range(NZ):
        columns = pl.ds((k % PER) * PIECE, PIECE)
        group = [pltpu.make_async_copy(other_hbm.at[k], other.at[k], sem.at[k, 0])]
        first = 0
        for i, part in enumerate(weights_hbm):
            rows = part.shape[0]
            group.append(
                pltpu.make_async_copy(
                    part.at[:, pl.ds(k * PIECE, PIECE)],
                    weight.at[k // PER, pl.ds(first, rows), columns],
                    sem.at[k, i + 1],
                )
            )
            first += rows
        for copy in group:
            copy.start()
        copies.append(group)
    for k in range(CHUNKS):
        pieces = range(k * PER, (k + 1) * PER)
        for i in pieces:
            for copy in copies[i]:
                copy.wait()
        for block, ref in enumerate((own_ref, other)):
            part = None
            for i in pieces:
                one = lax.dot_general(
                    ref[i], weight[k, :, (i % PER) * PIECE : (i % PER + 1) * PIECE], NT,
                    preferred_element_type=F32,
                )
                part = one if part is None else part + one
            if k == 0:
                acc[block * TOK : (block + 1) * TOK] = part
            else:
                acc[block * TOK : (block + 1) * TOK] += part


def query_kernel(own_ref, order_ref, other_hbm, *refs):
    weights_hbm, (out_ref, other, weight, acc, sem) = refs[:-5], refs[-5:]
    multiply(own_ref, other_hbm, weights_hbm, other, weight, acc, sem)
    rows = signs_and_order(acc[...], order_ref[...])
    for block in range(2):
        for s in range(2):
            out_ref[block, s] = rows[block * TOK : (block + 1) * TOK, s * HD : (s + 1) * HD]


def key_value_kernel(own_ref, order_ref, other_hbm, *refs):
    weights_hbm, (out_ref, state_ref, total_ref, other, weight, acc, sem) = refs[:-7], refs[-7:]
    multiply(own_ref, other_hbm, weights_hbm, other, weight, acc, sem)
    rows = signs_and_order(acc[...], order_ref[...])
    for s in range(2):
        for block in range(2):
            part = rows[block * TOK : (block + 1) * TOK]
            key = part[:, s * HD : (s + 1) * HD]
            value = part[:, (2 + s) * HD : (3 + s) * HD]
            out_ref[0, block, s] = key
            out_ref[1, block, s] = value
            state_ref[block, s] = lax.dot_general(key, value, TN, preferred_element_type=F32)
        total = (state_ref[0, s] + state_ref[1, s]).reshape(NX * NY // 2, 8, HD)
        total_ref[s * NX * NY // 2 : (s + 1) * NX * NY // 2] = total.astype(BF16)


def project(kernel, own, other, weights, order, out_shape):
    rows = sum(weight.shape[0] for weight in weights)
    vmem = pl.BlockSpec(memory_space=pltpu.VMEM)
    far = [pltpu.with_memory_space_constraint(a, pltpu.HBM) for a in (other, *weights)]
    return pl.pallas_call(
        kernel,
        in_specs=[vmem, vmem]
        + [pl.BlockSpec(memory_space=pltpu.HBM)] * len(far),
        out_specs=jax.tree.map(lambda s: vmem, out_shape),
        scratch_shapes=[
            pltpu.VMEM(other.shape, BF16),
            pltpu.VMEM((CHUNKS, rows, PER * PIECE), BF16),
            pltpu.VMEM((2 * TOK, rows), F32),
            pltpu.SemaphoreType.DMA((NZ, len(far))),
        ],
        out_shape=out_shape,
        compiler_params=pltpu.CompilerParams(vmem_limit_bytes=24 << 20),
    )(own, order, *far)


def prefix_kernel(total_ref, out_ref):
    run = jnp.zeros(total_ref.shape[1:], F32)
    for chip in range(NX * NY):
        out_ref[chip] = run.astype(BF16)
        run = run + total_ref[chip].astype(F32)


def inner_kernel(query_ref, kv_ref, out_ref):
    row = lax.broadcasted_iota(jnp.int32, (TOK, TOK), 0)
    col = lax.broadcasted_iota(jnp.int32, (TOK, TOK), 1)
    for block in range(2):
        for s in range(2):
            scores = lax.dot_general(
                query_ref[block, s], kv_ref[0, block, s], NT, preferred_element_type=F32
            )
            weights = jnp.where(col <= row, scores, 0.0).astype(BF16)
            out_ref[block, s] = jnp.dot(weights, kv_ref[1, block, s], preferred_element_type=F32)


def cross_kernel(query_ref, inner_ref, state_ref, prior_ref, mine_ref, theirs_ref):
    core = lax.axis_index("c")
    prior = prior_ref[...].astype(F32).reshape(2, HD, HD)
    for block, out_ref in enumerate((mine_ref, theirs_ref)):
        later = jnp.where(core == (1 - block), jnp.float32(1.0), jnp.float32(0.0))
        for s in range(2):
            carried = (prior[s] + later * state_ref[1 - block, s]).astype(BF16)
            combined = inner_ref[block, s] + jnp.dot(
                query_ref[block, s], carried, preferred_element_type=F32
            )
            scale = lax.rsqrt(jnp.mean(combined * combined, axis=-1, keepdims=True) + 1e-05)
            out_ref[s] = (combined * scale).astype(BF16)


def call(kernel, out_shape, *args, unread=0):
    spaces = [pltpu.VMEM] * (len(args) - unread) + [pltpu.HBM] * unread
    args = [
        pltpu.with_memory_space_constraint(arg, space) if space is pltpu.HBM else arg
        for arg, space in zip(args, spaces)
    ]
    return pl.pallas_call(
        kernel,
        out_shape=out_shape,
        in_specs=[pl.BlockSpec(memory_space=space) for space in spaces],
        out_specs=jax.tree.map(lambda s: pl.BlockSpec(memory_space=pltpu.VMEM), out_shape),
        compiler_params=pltpu.CompilerParams(vmem_limit_bytes=12 << 20),
    )(*args)


def shape(*dims, dtype=BF16):
    return jax.ShapeDtypeStruct(dims, dtype)


def on_device(hidden_in, proj_weights, directions):
    x, c = lax.axis_index("x"), lax.axis_index("c")
    swap = [(0, 1), (1, 0)]

    both = jnp.stack(
        [jnp.transpose(proj_weights, (0, 2, 3, 1)), jnp.transpose(directions, (0, 2, 3, 1))], axis=2
    )
    kv_rows = jnp.transpose(both[1:], (1, 0, 2, 3, 4)).reshape(NC, 8, D)
    q_rows = both[0].reshape(NC, 4, D)

    kv_part = exchange(replicate(kv_rows, NX).reshape(NX * NC, 8, D), ("x", "c"))
    kv_weight = lax.all_gather(kv_part.reshape(64, D), "y", axis=0, tiled=True)
    own = exchange(replicate(hidden_in, NZ), "z")

    q_first, q_second = q_rows[0], q_rows[1]
    q_mine = jnp.where(c == 0, q_first, q_second)
    q_theirs = lax.ppermute(jnp.where(c == 0, q_second, q_first), "c", swap)
    q_part = lax.all_gather(jnp.concatenate([q_mine, q_theirs]), "y", axis=0, tiled=True)
    up = [(i, (i + 1) % NX) for i in range(NX)]
    down = [(i, (i - 1) % NX) for i in range(NX)]
    q_after, q_before = lax.ppermute(q_part, "x", down), lax.ppermute(q_part, "x", up)
    own, q_after, q_before = lax.optimization_barrier((own, q_after, q_before))
    other = lax.ppermute(own, "c", swap)
    q_far = lax.ppermute(q_after, "x", down)
    q_weights = [q_part, q_after, q_far, q_before]

    query = project(
        query_kernel, own, other, q_weights, column_order(1, x, c), shape(2, 2, TOK, HD)
    )
    kv, state, total = project(
        key_value_kernel,
        own,
        other,
        [kv_weight],
        column_order(2),
        (shape(2, 2, 2, TOK, HD), shape(2, 2, HD, HD, dtype=F32), shape(NX * NY, 8, HD)),
    )

    totals, query = lax.optimization_barrier((exchange(total, ("x", "y")), query))
    slices = call(prefix_kernel, shape(NX * NY, 8, HD), totals)
    prior = exchange(slices, ("x", "y"))

    inner = call(inner_kernel, shape(2, 2, TOK, HD, dtype=F32), query, kv)
    block = shape(2, TOK, HD)
    mine, sent = call(cross_kernel, (block, block), query, inner, state, prior)
    theirs = lax.ppermute(sent, "c", swap)
    first = jnp.where(c == 0, mine, theirs)
    second = jnp.where(c == 0, theirs, mine)
    return jnp.stack([first, second], axis=2)


def solution(mesh):
    mesh4 = Mesh(mesh.devices.reshape(NX, NY, NC, NZ), ("x", "y", "c", "z"))
    ctx = ("x", "y", "c")
    return jax.shard_map(
        on_device,
        mesh=mesh4,
        in_specs=(P(ctx, "z"), P(None, None, "z", ctx), P(None, None, "z", ctx)),
        out_specs=P(None, ctx, "z", None),
        check_vma=False,
    )
```
